128 devices in a mesh: sec: 2 (over core), tile: 64 (over x, y, z).
Axes of the slice: x: 4, y: 4, z: 4, core: 2. Of those that a mesh axis runs over, the one named last changes fastest.
Arguments:
- atm_state: float32 [2, 32768, 4, 128], P('sec', 'tile'), may hold values from -8 to 8, as said below
- routes: int32 [2, 32768, 1], P('sec', 'tile'), may hold values from 0 to 63; in each aligned block of 512 rows (0 to 511, 512 to 1023, ..., all dimensions but the last counted through in order) at most 16 rows name the same one
- dst_block: int32 [2, 32768], P('sec', 'tile'), may hold values from 0 to 127
- weight_index: int32 [2, 32768], P('sec', 'tile'), may hold values from 0 to 15
- area_table: float32 [16, 128], replicated, may hold values from 0.1 to 1
- ocean_temp: float32 [2, 80, 1024, 1024], P('sec', None, 'tile'), may hold values from -6 to 6
- vel_u: float32 [2, 80, 1024, 1024], P('sec', None, 'tile'), may hold values from -0.6 to 0.6
- vel_v: float32 [2, 80, 1024, 1024], P('sec', None, 'tile'), may hold values from -0.6 to 0.6
- depth_levels: int32 [2, 1024, 1024], P('sec', 'tile'), may hold values from 0 to 80, as said below
Outputs:
- following_water_warmth: float32 [2, 80, 1024, 1024], P('sec', None, 'tile')
- coupler_skin_warmth: float32 [2, 32768, 128], P('sec', 'tile')
The draws below stay inside these ranges and needn't reach their ends.
Inputs may be any that keep to these rules, and one draw needn't show every extreme that they name: `routes`: among the 512 exchange blocks of one atmosphere device at most 16 map to one ocean tile, and exactly 16 do for some pair in every draw. `atm_state`: channel 0 (wind speed) lies in 0.5 to 4. `depth_levels`: about a quarter of the columns are land.
All inputs are finite; a program needn't handle non-finite values.
Results may differ from the reference program's by a relative error of at most 0.000071.
Values sent between devices are 32-bit elements; how exact they have to be, the bound alone decides.
No kernel may reach another device: no remote copies, remote signals or barrier semaphores. Data moves between devices by JAX's collectives and lax.ppermute only.
A program may use at most 256 MiB of HBM per device.

```python
import math
import jax
import jax.numpy as jnp
import numpy as np

NB = 512
PATCH_POINTS = 128
NW = 16
Z = 80
OX = 1024
C = 16
ATM_BLOCKS = 32768
NY = 1024
MARINE_PATCHES = 128
N_TILE = 64


def draw_atm_state(key, part):
    keys = jax.random.split(jax.random.fold_in(key, 11), 4)
    shape = (2, ATM_BLOCKS, PATCH_POINTS)
    speed = jnp.exp(jax.random.uniform(keys[0], shape, jnp.float32, math.log(0.5), math.log(4.0)))
    air = jnp.clip(jax.random.normal(keys[1], shape, jnp.float32), -4.0, 4.0)
    humidity = 0.5 * jnp.clip(jax.random.normal(keys[2], shape, jnp.float32), -4.0, 4.0)
    radiation = 0.3 + jnp.clip(jax.random.normal(keys[3], shape, jnp.float32), -4.0, 4.0)
    return jnp.stack([speed, air, humidity, radiation], axis=2)


def draw_depth_levels(key, part):
    drawn = jax.random.randint(jax.random.fold_in(key, 23), (2, NY, OX), -(Z // 3), Z + 1)
    return jnp.clip(drawn, 0, Z).astype(jnp.int32)


def set_ends(entries, stream_key, smallest, largest):
    dims = entries.shape
    spot = [jax.random.randint(jax.random.fold_in(stream_key, axis), (), 0, dims[axis]) for axis in range(len(dims))]
    entries = entries.at[tuple(spot)].set(smallest)
    longest = dims.index(max(dims))
    spot[longest] = (spot[longest] + 1) % dims[longest]
    return entries.at[tuple(spot)].set(largest)


def block_scale(rng, shape, shards, low, top_value):
    factor_of, own = 1.0, jax.random.fold_in(rng, 6)
    for axis_at, parts in shards:
        steps = jnp.exp(jax.random.uniform(jax.random.fold_in(own, axis_at), (parts,), jnp.float32, low / len(shards), top_value / len(shards)))
        factor_of = factor_of * jnp.repeat(steps, shape[axis_at] // parts).reshape([-1 if axis == axis_at else 1 for axis in range(len(shape))])
    return factor_of


def shared_out(key, own, number, rows, count, top, limit, lean):
    order = jax.random.permutation(key, count)
    packed, usual = portions_of(count, rows * top, limit, lean, True), portions_of(count, rows * top, limit, lean, False)
    places = jnp.arange(count)

    def named(sizes, turn):
        used = int((sizes > 0).sum())
        fixed = max(1, used // 4)
        shifted = fixed + (places - fixed + turn * (used - fixed)) % max(1, count - fixed)
        return jnp.zeros((count,), jnp.int32).at[order[jnp.where(places < fixed, places, shifted)]].set(jnp.asarray(sizes, jnp.int32))

    sizes = jnp.where(number % 4 == 0, named(packed, number // 4), named(usual, number - number // 4 - 1))
    mixed = jax.random.permutation(jax.random.fold_in(own, 3), count)
    donor, receiver = mixed[0:count // 2 * 2:2], mixed[1:count // 2 * 2:2]
    slack = jnp.minimum(sizes[donor] - 1, limit - sizes[receiver]) // 2
    slack = jnp.where((donor == order[0]) | (receiver == order[0]) | (sizes[receiver] == 0), 0, jnp.maximum(slack, 0))
    shifted = jax.random.randint(jax.random.fold_in(own, 4), (count // 2,), 0, 1 << 20) % (slack + 1)
    sizes = sizes.at[donor].add(-shifted).at[receiver].add(shifted)
    items = jnp.searchsorted(jnp.cumsum(sizes), jnp.arange(rows * top), side="right").astype(jnp.int32)
    listing = items.reshape(top, rows).T
    listing = listing[jax.random.permutation(jax.random.fold_in(own, 1), rows)]
    turn = jax.random.randint(jax.random.fold_in(own, 2), (rows, 1), 0, top)
    return jnp.take_along_axis(listing, (jnp.arange(top)[None, :] + turn) % top, axis=1)


def portions_of(number_of, total, limit, skew, full):
    weights = [(1 << 20) // math.isqrt(standing ** skew) + 1 for standing in range(1, number_of + 1)]
    largest = limit if full else min(limit, max(-(-total // number_of), total * weights[0] // sum(weights)))
    least = 1 if total - largest >= number_of - 1 else 0
    holding, spare = [largest] + [least] * (number_of - 1), total - largest - least * (number_of - 1)
    while spare > 0:
        candidates = [i for i in range(1, number_of) if holding[i] < largest] or [i for i in range(1, number_of) if holding[i] < limit]
        mass, remaining = sum([weights[i] for i in candidates]), spare
        for i in candidates:
            addition = min(limit - holding[i], max(1, remaining * weights[i] // mass), spare)
            holding[i] = holding[i] + addition
            spare = spare - addition
    return np.array(holding)


def centred(rng, extent, scale, bound, cuts=(), held_as=jnp.bfloat16):
    array = jax.random.normal(rng, extent, jnp.float32) * scale
    if len(cuts) > 0:
        array = block_scale(rng, extent, cuts, -0.22, 0.18) * array
    return jnp.clip(array, min=-bound, max=bound).astype(held_as)


def setup_inputs(seed: int = 0) -> dict:
    seeds = jax.random.split(jax.random.key(seed), 10)
    atm_state = draw_atm_state(jax.random.fold_in(seeds[9], 71), 0)
    routes_keys = jax.random.split(jax.random.fold_in(seeds[1], 1), 2 * ATM_BLOCKS // NB)
    routes_turns = jax.random.permutation(jax.random.fold_in(seeds[1], 3), 2 * ATM_BLOCKS // NB)
    routes = jax.vmap(lambda own, number: shared_out(jax.random.fold_in(seeds[1], 2), own, number, NB, N_TILE, 1, C, 2))(routes_keys, routes_turns).reshape((2, ATM_BLOCKS, 1))
    dst_block = set_ends(jax.random.randint(seeds[2], (2, ATM_BLOCKS), 0, MARINE_PATCHES), jax.random.fold_in(seeds[2], 1), 0, MARINE_PATCHES - 1).astype(jnp.int32)
    weight_index = set_ends(jax.random.randint(seeds[3], (2, ATM_BLOCKS), 0, NW), jax.random.fold_in(seeds[3], 1), 0, NW - 1).astype(jnp.int32)
    area_table = jnp.clip(jnp.exp(jax.random.uniform(seeds[4], (NW, PATCH_POINTS), jnp.float32, math.log(0.1), math.log(1.0))), 0.1, 1.0)
    ocean_temp = centred(seeds[5], (2, Z, NY, OX), 1.0, 6.0, ((0, 2), (2, 64)), jnp.float32)
    vel_u = centred(seeds[6], (2, Z, NY, OX), 0.15, 0.6, ((0, 2), (2, 64)), jnp.float32)
    vel_v = centred(seeds[7], (2, Z, NY, OX), 0.15, 0.6, ((0, 2), (2, 64)), jnp.float32)
    depth_levels = draw_depth_levels(jax.random.fold_in(seeds[9], 71), 0)
    return dict(atm_state=atm_state, routes=routes, dst_block=dst_block, weight_index=weight_index, area_table=area_table, ocean_temp=ocean_temp, vel_u=vel_u, vel_v=vel_v, depth_levels=depth_levels)


heat_diffusion = 0.12
vertical_mixing = 0.2
flux_gain = 0.5


def bulk_flux(state, surface_temp):
    speed = state[..., 0, :]
    air = state[..., 1, :]
    humidity = state[..., 2, :]
    radiation = state[..., 3, :]
    contrast = surface_temp - air
    transfer = 0.8 + 0.4 * jnp.tanh(contrast)
    saturation = 0.6 * jnp.exp(0.3 * surface_temp)
    return radiation - transfer * speed * (contrast + 1.5 * (saturation - humidity))


def march_forward(padded_field, driving_heat_input):
    field = padded_field[0]
    zonal = padded_field[1]
    meridional = padded_field[2]
    wetness = padded_field[3]
    centre = field[:, 1:-1]
    wet_c = wetness[:, 1:-1]
    zonal_c = zonal[:, 1:-1]
    merid_c = meridional[:, 1:-1]
    east = jnp.roll(centre, -1, axis=2)
    west = jnp.roll(centre, 1, axis=2)
    wet_e = jnp.roll(wet_c, -1, axis=2)
    wet_w = jnp.roll(wet_c, 1, axis=2)
    north = field[:, 2:]
    south = field[:, :-2]
    wet_n = wetness[:, 2:]
    wet_s = wetness[:, :-2]
    flux_east = 0.25 * (zonal_c + jnp.roll(zonal_c, -1, axis=2)) * (centre + east) * wet_c * wet_e
    flux_west = jnp.roll(flux_east, 1, axis=2)
    flux_north = 0.25 * (merid_c + meridional[:, 2:]) * (centre + north) * wet_c * wet_n
    flux_south = 0.25 * (meridional[:, :-2] + merid_c) * (south + centre) * wet_s * wet_c
    spread = heat_diffusion * (wet_e * (east - centre) + wet_w * (west - centre) + wet_n * (north - centre) + wet_s * (south - centre))
    above = jnp.pad(centre[:-1], ((1, 0), (0, 0), (0, 0)))
    below = jnp.pad(centre[1:], ((0, 1), (0, 0), (0, 0)))
    wet_above = jnp.pad(wet_c[:-1], ((1, 0), (0, 0), (0, 0)))
    wet_below = jnp.pad(wet_c[1:], ((0, 1), (0, 0), (0, 0)))
    mixing = vertical_mixing * (wet_above * (above - centre) + wet_below * (below - centre))
    tendency = spread + mixing - (flux_east - flux_west) - (flux_north - flux_south)
    surface = jnp.concatenate([(flux_gain * driving_heat_input)[None], jnp.zeros_like(centre[1:])], axis=0)
    return centre + wet_c * (tendency + surface)


def reference(atm_state, routes, dst_block, weight_index, area_table, ocean_temp, vel_u, vel_v, depth_levels):
    state = atm_state[0]
    dest_tile = routes[0, :, 0]
    block_id = dst_block[0]
    table_row = weight_index[0]
    temp = ocean_temp[1]
    levels = depth_levels[1]
    wetness = (jnp.arange(Z, dtype=jnp.int32)[:, None, None] < levels[None]).astype(jnp.float32)
    top = temp[0].reshape(N_TILE * MARINE_PATCHES, PATCH_POINTS)
    destination_patch = (dest_tile * MARINE_PATCHES + block_id).astype(jnp.int32)
    surface = top[destination_patch]
    heat = bulk_flux(state, surface)
    weights = area_table[table_row]
    heat_sum = jnp.zeros((N_TILE * MARINE_PATCHES, PATCH_POINTS), jnp.float32).at[destination_patch].add(weights * heat)
    area_sum = jnp.zeros((N_TILE * MARINE_PATCHES, PATCH_POINTS), jnp.float32).at[destination_patch].add(weights)
    driving_heat_input = (heat_sum / jnp.maximum(area_sum, 1.0)).reshape(NY, OX)
    stacked = jnp.stack([temp, vel_u[1], vel_v[1], wetness])
    padded_field = jnp.pad(stacked, ((0, 0), (0, 0), (1, 1), (0, 0)))
    revised_warmth = march_forward(padded_field, driving_heat_input)
    marine_skin_warmth = revised_warmth[0].reshape(N_TILE * MARINE_PATCHES, PATCH_POINTS)[destination_patch]
    following_water_warmth = jnp.stack([jnp.zeros_like(revised_warmth), revised_warmth])
    coupler_skin_warmth = jnp.stack([marine_skin_warmth, jnp.zeros_like(marine_skin_warmth)])
    return following_water_warmth, coupler_skin_warmth
```

```python
import functools

import jax
import jax.numpy as jnp
from jax import lax
from jax.experimental import pallas as pl
from jax.experimental.pallas import tpu as pltpu
from jax.sharding import PartitionSpec as P

HEAT_DIFFUSION = 0.12
VERTICAL_MIXING = 0.2
FLUX_GAIN = 0.5
CAPACITY = 16
CHUNK = CAPACITY + 2
UNROLL = 8
LEVELS = 8

f32, bf16, i32 = jnp.float32, jnp.bfloat16, jnp.int32
VMEM = pl.BlockSpec(memory_space=pltpu.VMEM)
SMEM = pl.BlockSpec(memory_space=pltpu.SMEM)
ANY = pl.BlockSpec(memory_space=pl.ANY)


def iota(shape, axis):
    return lax.broadcasted_iota(i32, shape, axis)


def pack_kernel(
    tiles, sec, dest, block, row, state, depth, temp, merid,
    payload, slot_of, up, down,
    count, entry, edge, sem,
):
    levels = temp.shape[1]
    rows = temp.shape[2]

    @pl.when(sec[0] == 0)
    def _():
        def clear(i, _):
            count[i] = 0
            return 0

        lax.fori_loop(0, tiles, clear, 0)
        entry[...] = jnp.full(entry.shape, -1.0, f32)
        is_block = (iota((1, 128), 1) & 32) == 0

        def place(step, _):
            for j in range(UNROLL):
                i = step * UNROLL + j
                d = dest[i]
                c = count[d]
                count[d] = c + 1
                c = jnp.minimum(c, CAPACITY - 1)
                slot = d * CAPACITY + c
                slot_of[i] = slot
                payload[d * CHUNK + c] = state[0, i]
                entry[pl.ds(slot, 1), :] = jnp.where(is_block, block[i], row[i]).astype(f32)
            return 0

        lax.fori_loop(0, dest.shape[0] // UNROLL, place, 0)
        left = iota((8, 128), 1) < 64

        def entries_of(d, _):
            low = entry[pl.ds(pl.multiple_of(d * CAPACITY, 8), 8), :]
            high = entry[pl.ds(pl.multiple_of(d * CAPACITY + 8, 8), 8), :]
            both = jnp.where(left, low, high)
            payload[d * CHUNK + CAPACITY] = both[0:4]
            payload[d * CHUNK + CAPACITY + 1] = both[4:8]
            return 0

        lax.fori_loop(0, tiles, entries_of, 0)

    @pl.when(sec[0] != 0)
    def _():
        def none(i, _):
            slot_of[i] = 0
            return 0

        lax.fori_loop(0, dest.shape[0], none, 0)
        copies = []
        for n, (field, lo) in enumerate(
            ((temp, rows - 8), (merid, rows - 8), (temp, 0), (merid, 0))
        ):
            copies.append(
                pltpu.make_async_copy(field.at[0, :, pl.ds(lo, 8), :], edge.at[n], sem.at[n])
            )
        for copy in copies:
            copy.start()
        up[2 * levels :, :] = jnp.broadcast_to(
            depth[0, rows - 1 :, :].astype(f32), (8, depth.shape[2])
        )
        down[2 * levels :, :] = jnp.broadcast_to(
            depth[0, 0:1, :].astype(f32), (8, depth.shape[2])
        )
        for n, copy in enumerate(copies):
            copy.wait()
            target = up if n < 2 else down
            target[pl.ds((n % 2) * levels, levels), :] = edge[n, :, 7 if n < 2 else 0, :]


def ocean_kernel(
    levels, sec, temp, beneath, zonal, merid, depth, south, north,
    out, top,
    depth_e, depth_n, depth_s, carry,
):
    step = pl.program_id(0)
    rows, cells = depth.shape[1:]

    @pl.when(sec[0] == 0)
    def _():
        out[...] = jnp.zeros_like(out)

        @pl.when(step == 0)
        def _():
            top[...] = jnp.zeros_like(top)

    @pl.when(sec[0] != 0)
    def _():
        first = iota((rows, cells), 0) == 0
        last = iota((rows, cells), 0) == rows - 1

        @pl.when(step == 0)
        def _():
            d = depth[0]
            depth_e[...] = jnp.minimum(d, pltpu.roll(d, cells - 1, 1))
            d_north = north[2 * levels : 2 * levels + 1, :].astype(i32)
            d_south = south[2 * levels : 2 * levels + 1, :].astype(i32)
            depth_n[...] = jnp.minimum(d, jnp.where(last, d_north, pltpu.roll(d, rows - 1, 0)))
            depth_s[...] = jnp.broadcast_to(jnp.minimum(d[0:1], d_south), depth_s.shape)
            carry[...] = jnp.zeros_like(carry)

        above = carry[...]
        for j in range(LEVELS):
            k = step * LEVELS + j
            t = temp[0, j]
            u = zonal[0, j]
            v = merid[0, j]
            t_e = pltpu.roll(t, cells - 1, 1)
            u_e = pltpu.roll(u, cells - 1, 1)
            east = jnp.where(
                k < depth_e[...],
                HEAT_DIFFUSION * (t_e - t) - (0.25 * (u + u_e)) * (t + t_e),
                0.0,
            )
            t_n = jnp.where(last, north[pl.ds(k, 1), :], pltpu.roll(t, rows - 1, 0))
            v_n = jnp.where(last, north[pl.ds(levels + k, 1), :], pltpu.roll(v, rows - 1, 0))
            northward = jnp.where(
                k < depth_n[...],
                HEAT_DIFFUSION * (t_n - t) - (0.25 * (v + v_n)) * (t + t_n),
                0.0,
            )
            t_s = south[pl.ds(k, 1), :]
            v_s = south[pl.ds(levels + k, 1), :]
            t_0 = t[0:1]
            southmost = jnp.where(
                k < depth_s[0:1, :],
                HEAT_DIFFUSION * (t_0 - t_s) - (0.25 * (v[0:1] + v_s)) * (t_0 + t_s),
                0.0,
            )
            under = beneath[0, 0] if j == LEVELS - 1 else temp[0, j + 1]
            below = jnp.where(k + 1 < depth[0], VERTICAL_MIXING * (under - t), 0.0)
            fresh = (
                t
                + (east - pltpu.roll(east, 1, 1))
                + (northward - jnp.where(first, southmost, pltpu.roll(northward, 1, 0)))
                + (below - above)
            )
            above = below
            out[0, j] = fresh
            if j == 0:

                @pl.when(step == 0)
                def _():
                    wet = jnp.where(depth[0] > 0, FLUX_GAIN, 0.0)
                    patches = cells // 128
                    for p in range(patches):
                        part = slice(p * 128, p * 128 + 128)
                        top[0, pl.ds(p, rows, stride=patches), :] = t[:, part]
                        top[1, pl.ds(p, rows, stride=patches), :] = fresh[:, part]
                        top[2, pl.ds(p, rows, stride=patches), :] = wet[:, part]

        carry[...] = above


def in_three(x):
    high = x.astype(bf16)
    rest = x - high.astype(f32)
    middle = rest.astype(bf16)
    low = (rest - middle.astype(f32)).astype(bf16)
    return jnp.concatenate([high, middle, low], axis=1)


def joined(x, at=0):
    return x[:, at : at + 128] + (x[:, at + 128 : at + 256] + x[:, at + 256 : at + 384])


def heat_kernel(tiles, sec, payload, top, table, ret, fresh, hit, weighted):
    slots = tiles * CAPACITY

    @pl.when(sec[0] != 0)
    def _():
        ret[...] = jnp.zeros_like(ret)
        fresh[...] = jnp.zeros_like(fresh)

    @pl.when(sec[0] == 0)
    def _():
        surface_parts = in_three(top[0])
        table_parts = in_three(
            jnp.concatenate([table[...], jnp.zeros((128 - table.shape[0], 128), f32)], axis=0)
        )
        lane = iota((1, 8, 128), 2).astype(f32)
        group = 8

        def step(g, _):
            base = pl.multiple_of(g * group, group)
            upper = payload[pl.ds(base * CHUNK, group * CHUNK)].reshape(group, CHUNK, 4, 128)
            entry = upper[:, CAPACITY:].reshape(group, 8, 128)
            at = pl.multiple_of(base * CAPACITY, group * CAPACITY)
            size = group * CAPACITY
            block_hit = jnp.concatenate(
                [entry[:, None, :, 0:1] == lane[None], entry[:, None, :, 64:65] == lane[None]],
                axis=1,
            ).reshape(size, 128)
            row_hit = jnp.concatenate(
                [entry[:, None, :, 32:33] == lane[None], entry[:, None, :, 96:97] == lane[None]],
                axis=1,
            ).reshape(size, 128)
            live = jnp.concatenate(
                [
                    jnp.broadcast_to(entry[:, None, :, 0:1], (group, 1, 8, 128)),
                    jnp.broadcast_to(entry[:, None, :, 64:65], (group, 1, 8, 128)),
                ],
                axis=1,
            ).reshape(size, 128) >= 0
            block_one = jnp.where(block_hit, 1.0, 0.0).astype(bf16)
            row_one = jnp.where(row_hit, 1.0, 0.0).astype(bf16)
            hit[pl.ds(at, size), :] = block_one
            surface = joined(jnp.dot(block_one, surface_parts, preferred_element_type=f32))
            weights = joined(jnp.dot(row_one, table_parts, preferred_element_type=f32))

            def channel(c):
                return upper[:, :CAPACITY, c, :].reshape(size, 128)

            contrast = surface - channel(1)
            transfer = 0.8 + 0.4 * jnp.tanh(contrast)
            saturation = 0.6 * jnp.exp(0.3 * surface)
            heat = channel(3) - transfer * channel(0) * (
                contrast + 1.5 * (saturation - channel(2))
            )
            product = jnp.where(live, weights * heat, 0.0)
            weighted[pl.ds(at, size), 0:384] = in_three(product)
            weighted[pl.ds(at, size), 384:768] = in_three(weights)
            return 0

        lax.fori_loop(0, tiles // group, step, 0)
        sums = lax.dot_general(
            hit[...], weighted[...], (((0,), (0,)), ((), ())), preferred_element_type=f32
        )
        forcing = joined(sums) / jnp.maximum(joined(sums, 384), 1.0)
        new_top = top[1] + top[2] * forcing
        fresh[...] = new_top
        ret[...] = joined(jnp.dot(hit[...], in_three(new_top), preferred_element_type=f32))


def settle_kernel(fresh, whole, out):
    rows, cells = out.shape[2:]
    patches = cells // 128
    for p in range(patches):
        out[0, 0, :, p * 128 : p * 128 + 128] = fresh[pl.ds(p, rows, stride=patches), :]


def body(
    atm_state, routes, dst_block, weight_index, area_table, ocean_temp, vel_u, vel_v, depth_levels
):
    tiles = lax.axis_size("tile")
    block_count = atm_state.shape[1]
    levels, rows, cells = ocean_temp.shape[1:]
    patches = rows * cells // 128
    slots = tiles * CAPACITY
    sec = lax.axis_index("sec").astype(i32).reshape(1)
    grant = pltpu.CompilerParams(vmem_limit_bytes=48 << 20)

    edge_rows = 2 * levels + 8
    payload, slot_of, up, down = pl.pallas_call(
        functools.partial(pack_kernel, tiles),
        out_shape=(
            jax.ShapeDtypeStruct((tiles * CHUNK, 4, 128), f32),
            jax.ShapeDtypeStruct((block_count,), i32),
            jax.ShapeDtypeStruct((edge_rows, cells), f32),
            jax.ShapeDtypeStruct((edge_rows, cells), f32),
        ),
        in_specs=[SMEM, SMEM, SMEM, SMEM, VMEM, VMEM, ANY, ANY],
        out_specs=(VMEM, SMEM, VMEM, VMEM),
        scratch_shapes=[
            pltpu.SMEM((tiles,), i32),
            pltpu.VMEM((slots, 128), f32),
            pltpu.VMEM((4, levels, 8, cells), f32),
            pltpu.SemaphoreType.DMA((4,)),
        ],
        compiler_params=grant,
        name="pack",
    )(
        sec, routes.reshape(block_count), dst_block.reshape(block_count),
        weight_index.reshape(block_count), atm_state, depth_levels, ocean_temp, vel_v,
    )

    north_to = [(tiles + t, tiles + t + 1) for t in range(tiles - 1)]
    south_to = [(t + 1, t) for t in range(tiles, 2 * tiles - 1)]
    south = lax.ppermute(up, ("sec", "tile"), north_to)
    north = lax.ppermute(down, ("sec", "tile"), south_to)
    moved = lax.all_to_all(payload, "tile", split_axis=0, concat_axis=0, tiled=True)

    steps = levels // LEVELS
    slab = pl.BlockSpec((1, LEVELS, rows, cells), lambda i: (0, i, 0, 0))
    fixed3 = pl.BlockSpec((1, rows, cells), lambda i: (0, 0, 0))
    fixed2 = pl.BlockSpec((edge_rows, cells), lambda i: (0, 0))
    out, top = pl.pallas_call(
        functools.partial(ocean_kernel, levels),
        grid=(steps,),
        out_shape=(
            jax.ShapeDtypeStruct(ocean_temp.shape, f32),
            jax.ShapeDtypeStruct((3, patches, 128), f32),
        ),
        in_specs=[
            SMEM,
            slab,
            pl.BlockSpec(
                (1, 1, rows, cells),
                lambda i: (0, jnp.minimum((i + 1) * LEVELS, levels - 1), 0, 0),
            ),
            slab,
            slab,
            fixed3,
            fixed2,
            fixed2,
        ],
        out_specs=(slab, pl.BlockSpec((3, patches, 128), lambda i: (0, 0, 0))),
        scratch_shapes=[
            pltpu.VMEM((rows, cells), i32),
            pltpu.VMEM((rows, cells), i32),
            pltpu.VMEM((8, cells), i32),
            pltpu.VMEM((rows, cells), f32),
        ],
        compiler_params=grant,
        cost_estimate=pl.CostEstimate(
            flops=40 * levels * rows * cells,
            bytes_accessed=17 * levels * rows * cells,
            transcendentals=0,
        ),
        name="ocean",
    )(sec, ocean_temp, ocean_temp, vel_u, vel_v, depth_levels, south, north)
    top = lax.ppermute(top, "sec", [(1, 0)])

    ret, fresh = pl.pallas_call(
        functools.partial(heat_kernel, tiles),
        out_shape=(
            jax.ShapeDtypeStruct((slots, 128), f32),
            jax.ShapeDtypeStruct((patches, 128), f32),
        ),
        in_specs=[SMEM, VMEM, VMEM, VMEM],
        out_specs=(VMEM, VMEM),
        scratch_shapes=[pltpu.VMEM((slots, 128), bf16), pltpu.VMEM((slots, 768), bf16)],
        compiler_params=grant,
        name="heat",
    )(sec, moved, top, area_table)

    fresh = lax.ppermute(fresh, "sec", [(0, 1)])
    back = lax.all_to_all(ret, "tile", split_axis=0, concat_axis=0, tiled=True)
    level = pl.BlockSpec((1, 1, rows, cells), lambda i: (0, 0, 0, 0))
    following = pl.pallas_call(
        settle_kernel,
        grid=(1,),
        out_shape=jax.ShapeDtypeStruct(out.shape, f32),
        in_specs=[pl.BlockSpec((patches, 128), lambda i: (0, 0)), ANY],
        out_specs=level,
        input_output_aliases={1: 0},
        name="settle",
    )(fresh, out)
    skin = back.at[slot_of].get(mode="promise_in_bounds")
    return following, skin[None]


def solution(mesh):
    return jax.shard_map(
        body,
        mesh=mesh,
        in_specs=(
            P("sec", "tile", None, None),
            P("sec", "tile", None),
            P("sec", "tile"),
            P("sec", "tile"),
            P(),
            P("sec", None, "tile", None),
            P("sec", None, "tile", None),
            P("sec", None, "tile", None),
            P("sec", "tile", None),
        ),
        out_specs=(P("sec", None, "tile", None), P("sec", "tile", None)),
        check_vma=False,
    )
```

```python
import functools

import jax
import jax.numpy as jnp
from jax import lax
from jax.experimental import pallas as pl
from jax.experimental.pallas import tpu as pltpu
from jax.sharding import PartitionSpec as P

HEAT_DIFFUSION = 0.12
VERTICAL_MIXING = 0.2
FLUX_GAIN = 0.5
CAPACITY = 16
CHUNK = CAPACITY + 2
UNROLL = 8
LEVELS = 8

f32, bf16, i32 = jnp.float32, jnp.bfloat16, jnp.int32
VMEM = pl.BlockSpec(memory_space=pltpu.VMEM)
SMEM = pl.BlockSpec(memory_space=pltpu.SMEM)
ANY = pl.BlockSpec(memory_space=pl.ANY)
HBM = pl.BlockSpec(memory_space=pltpu.HBM)


def iota(shape, axis):
    return lax.broadcasted_iota(i32, shape, axis)


def pack_kernel(
    tiles, sec, dest_in, block_in, row_in, state_in, depth_in, temp, merid,
    payload_out, slot_of, up_out, down_out,
    dest, block, row, state, payload, count, entry, edge, depth, up, down,
    index_sem, state_sem, edge_sem, out_sem,
):
    levels = temp.shape[1]
    rows = temp.shape[2]
    blocks = dest.shape[0]
    pieces = state_sem.shape[0]
    piece = blocks // pieces

    @pl.when(sec[0] == 0)
    def _():
        indices = [
            pltpu.make_async_copy(source, target, index_sem.at[n])
            for n, (source, target) in enumerate(
                ((dest_in, dest), (block_in, block), (row_in, row))
            )
        ]
        states = [
            pltpu.make_async_copy(
                state_in.at[0, pl.ds(n * piece, piece)],
                state.at[pl.ds(n * piece, piece)],
                state_sem.at[n],
            )
            for n in range(pieces)
        ]
        for copy in indices + states:
            copy.start()

        for i in range(tiles):
            count[i] = 0
        entry[...] = jnp.full(entry.shape, -1.0, f32)
        is_block = (iota((1, 128), 1) & 32) == 0
        for copy in indices:
            copy.wait()

        def place(step, _):
            for j in range(UNROLL):
                i = step * UNROLL + j
                d = dest[i]
                c = count[d]
                count[d] = c + 1
                c = jnp.minimum(c, CAPACITY - 1)
                slot = d * CAPACITY + c
                slot_of[i] = slot
                payload[d * CHUNK + c] = state[i]
                entry[pl.ds(slot, 1), :] = jnp.where(is_block, block[i], row[i]).astype(f32)
            return 0

        for n in range(pieces):
            states[n].wait()
            lax.fori_loop(n * piece // UNROLL, (n + 1) * piece // UNROLL, place, 0)
        left = iota((8, 128), 1) < 64

        def entries_of(g, _):
            for j in range(8):
                d = g * 8 + j
                low = entry[pl.ds(pl.multiple_of(d * CAPACITY, 8), 8), :]
                high = entry[pl.ds(pl.multiple_of(d * CAPACITY + 8, 8), 8), :]
                both = jnp.where(left, low, high)
                payload[d * CHUNK + CAPACITY] = both[0:4]
                payload[d * CHUNK + CAPACITY + 1] = both[4:8]
            return 0

        lax.fori_loop(0, tiles // 8, entries_of, 0)
        half = payload.shape[0] // 2
        outs = [
            pltpu.make_async_copy(
                payload.at[pl.ds(n * half, half)], payload_out.at[pl.ds(n * half, half)], out_sem.at[n]
            )
            for n in range(2)
        ]
        for copy in outs:
            copy.start()
        for copy in outs:
            copy.wait()

    @pl.when(sec[0] != 0)
    def _():
        bring = pltpu.make_async_copy(depth_in.at[0], depth, index_sem.at[0])
        bring.start()
        copies = [
            pltpu.make_async_copy(field.at[0, :, pl.ds(lo, 8), :], edge.at[n], edge_sem.at[n])
            for n, (field, lo) in enumerate(
                ((temp, rows - 8), (merid, rows - 8), (temp, 0), (merid, 0))
            )
        ]
        for copy in copies:
            copy.start()

        def none(step, _):
            for j in range(UNROLL):
                slot_of[step * UNROLL + j] = 0
            return 0

        lax.fori_loop(0, blocks // UNROLL, none, 0)
        bring.wait()
        cells = depth.shape[1]
        up[2 * levels :, :] = jnp.broadcast_to(depth[rows - 1 :, :].astype(f32), (8, cells))
        down[2 * levels :, :] = jnp.broadcast_to(depth[0:1, :].astype(f32), (8, cells))
        for n, copy in enumerate(copies):
            copy.wait()
            target = up if n < 2 else down
            target[pl.ds((n % 2) * levels, levels), :] = edge[n, :, 7 if n < 2 else 0, :]
        outs = [
            pltpu.make_async_copy(up, up_out, out_sem.at[0]),
            pltpu.make_async_copy(down, down_out, out_sem.at[1]),
        ]
        for copy in outs:
            copy.start()
        for copy in outs:
            copy.wait()


def faces(levels, k, t, u, v, north, south, depth_e, depth_n, depth_s):
    rows, cells = t.shape
    first = iota((rows, cells), 0) == 0
    last = iota((rows, cells), 0) == rows - 1
    t_e = pltpu.roll(t, cells - 1, 1)
    u_e = pltpu.roll(u, cells - 1, 1)
    east = jnp.where(
        k < depth_e,
        HEAT_DIFFUSION * (t_e - t) - (0.25 * (u + u_e)) * (t + t_e),
        0.0,
    )
    t_n = jnp.where(last, north[pl.ds(k, 1), :], pltpu.roll(t, rows - 1, 0))
    v_n = jnp.where(last, north[pl.ds(levels + k, 1), :], pltpu.roll(v, rows - 1, 0))
    northward = jnp.where(
        k < depth_n,
        HEAT_DIFFUSION * (t_n - t) - (0.25 * (v + v_n)) * (t + t_n),
        0.0,
    )
    t_s = south[pl.ds(k, 1), :]
    v_s = south[pl.ds(levels + k, 1), :]
    t_0 = t[0:1]
    southmost = jnp.where(
        k < depth_s,
        HEAT_DIFFUSION * (t_0 - t_s) - (0.25 * (v[0:1] + v_s)) * (t_0 + t_s),
        0.0,
    )
    return (east - pltpu.roll(east, 1, 1)) + (
        northward - jnp.where(first, southmost, pltpu.roll(northward, 1, 0))
    )


def face_depths(levels, d, north, south):
    rows, cells = d.shape
    last = iota((rows, cells), 0) == rows - 1
    d_north = north[2 * levels : 2 * levels + 1, :].astype(i32)
    d_south = south[2 * levels : 2 * levels + 1, :].astype(i32)
    return (
        jnp.minimum(d, pltpu.roll(d, cells - 1, 1)),
        jnp.minimum(d, jnp.where(last, d_north, pltpu.roll(d, rows - 1, 0))),
        jnp.minimum(d[0:1], d_south),
    )


def surface_kernel(levels, sec, temp, zonal, merid, depth, south, north, top):
    @pl.when(sec[0] != 0)
    def _():
        d = depth[0]
        rows, cells = d.shape
        t = temp[0, 0]
        below = jnp.where(1 < d, VERTICAL_MIXING * (temp[0, 1] - t), 0.0)
        base = t + faces(
            levels, 0, t, zonal[0, 0], merid[0, 0], north, south,
            *face_depths(levels, d, north, south),
        ) + below
        wet = jnp.where(d > 0, FLUX_GAIN, 0.0)
        patches = cells // 128
        for p in range(patches):
            part = slice(p * 128, p * 128 + 128)
            top[0, pl.ds(p, rows, stride=patches), :] = t[:, part]
            top[1, pl.ds(p, rows, stride=patches), :] = base[:, part]
            top[2, pl.ds(p, rows, stride=patches), :] = wet[:, part]


def ocean_kernel(
    levels, sec, temp, beneath, zonal, merid, depth, south, north,
    out,
    depth_e, depth_n, depth_s, carry,
):
    step = pl.program_id(0)

    @pl.when(sec[0] == 0)
    def _():
        out[...] = jnp.zeros_like(out)

    @pl.when(sec[0] != 0)
    def _():
        @pl.when(step == 0)
        def _():
            e, n, s = face_depths(levels, depth[0], north, south)
            depth_e[...] = e
            depth_n[...] = n
            depth_s[...] = jnp.broadcast_to(s, depth_s.shape)
            carry[...] = jnp.zeros_like(carry)

        above = carry[...]
        for j in range(LEVELS):
            k = step * LEVELS + j
            t = temp[0, j]
            under = beneath[0, 0] if j == LEVELS - 1 else temp[0, j + 1]
            below = jnp.where(k + 1 < depth[0], VERTICAL_MIXING * (under - t), 0.0)
            out[0, j] = (
                t
                + faces(
                    levels, k, t, zonal[0, j], merid[0, j], north, south,
                    depth_e[...], depth_n[...], depth_s[0:1, :],
                )
                + (below - above)
            )
            above = below
        carry[...] = above


def in_three(x):
    high = x.astype(bf16)
    rest = x - high.astype(f32)
    middle = rest.astype(bf16)
    low = (rest - middle.astype(f32)).astype(bf16)
    return jnp.concatenate([high, middle, low], axis=1)


def joined(x, at=0):
    return x[:, at : at + 128] + (x[:, at + 128 : at + 256] + x[:, at + 256 : at + 384])


def heat_kernel(tiles, sec, payload, top, table, ret, fresh, hit, weighted):
    slots = tiles * CAPACITY

    @pl.when(sec[0] != 0)
    def _():
        ret[...] = jnp.zeros_like(ret)
        fresh[...] = jnp.zeros_like(fresh)

    @pl.when(sec[0] == 0)
    def _():
        surface_parts = in_three(top[0])
        table_parts = in_three(
            jnp.concatenate([table[...], jnp.zeros((128 - table.shape[0], 128), f32)], axis=0)
        )
        lane = iota((1, 8, 128), 2).astype(f32)
        group = 8

        def step(g, _):
            base = pl.multiple_of(g * group, group)
            upper = payload[pl.ds(base * CHUNK, group * CHUNK)].reshape(group, CHUNK, 4, 128)
            entry = upper[:, CAPACITY:].reshape(group, 8, 128)
            at = pl.multiple_of(base * CAPACITY, group * CAPACITY)
            size = group * CAPACITY
            block_hit = jnp.concatenate(
                [entry[:, None, :, 0:1] == lane[None], entry[:, None, :, 64:65] == lane[None]],
                axis=1,
            ).reshape(size, 128)
            row_hit = jnp.concatenate(
                [entry[:, None, :, 32:33] == lane[None], entry[:, None, :, 96:97] == lane[None]],
                axis=1,
            ).reshape(size, 128)
            live = jnp.concatenate(
                [
                    jnp.broadcast_to(entry[:, None, :, 0:1], (group, 1, 8, 128)),
                    jnp.broadcast_to(entry[:, None, :, 64:65], (group, 1, 8, 128)),
                ],
                axis=1,
            ).reshape(size, 128) >= 0
            block_one = jnp.where(block_hit, 1.0, 0.0).astype(bf16)
            row_one = jnp.where(row_hit, 1.0, 0.0).astype(bf16)
            hit[pl.ds(at, size), :] = block_one
            surface = joined(jnp.dot(block_one, surface_parts, preferred_element_type=f32))
            weights = joined(jnp.dot(row_one, table_parts, preferred_element_type=f32))

            def channel(c):
                return upper[:, :CAPACITY, c, :].reshape(size, 128)

            contrast = surface - channel(1)
            transfer = 0.8 + 0.4 * jnp.tanh(contrast)
            saturation = 0.6 * jnp.exp(0.3 * surface)
            heat = channel(3) - transfer * channel(0) * (
                contrast + 1.5 * (saturation - channel(2))
            )
            product = jnp.where(live, weights * heat, 0.0)
            weighted[pl.ds(at, size), 0:384] = in_three(product)
            weighted[pl.ds(at, size), 384:768] = in_three(weights)
            return 0

        lax.fori_loop(0, tiles // group, step, 0)
        sums = lax.dot_general(
            hit[...], weighted[...], (((0,), (0,)), ((), ())), preferred_element_type=f32
        )
        forcing = joined(sums) / jnp.maximum(joined(sums, 384), 1.0)
        new_top = top[1] + top[2] * forcing
        fresh[...] = new_top
        ret[...] = joined(jnp.dot(hit[...], in_three(new_top), preferred_element_type=f32))


def settle_kernel(fresh, whole, out):
    rows, cells = out.shape[2:]
    patches = cells // 128
    for p in range(patches):
        out[0, 0, :, p * 128 : p * 128 + 128] = fresh[pl.ds(p, rows, stride=patches), :]


def body(
    atm_state, routes, dst_block, weight_index, area_table, ocean_temp, vel_u, vel_v, depth_levels
):
    tiles = lax.axis_size("tile")
    block_count = atm_state.shape[1]
    levels, rows, cells = ocean_temp.shape[1:]
    patches = rows * cells // 128
    slots = tiles * CAPACITY
    sec = lax.axis_index("sec").astype(i32).reshape(1)
    grant = pltpu.CompilerParams(vmem_limit_bytes=24 << 20)
    ocean_grant = pltpu.CompilerParams(vmem_limit_bytes=56 << 20)
    whole_grant = pltpu.CompilerParams(vmem_limit_bytes=60 << 20)

    edge_rows = 2 * levels + 8
    payload, slot_of, up, down = pl.pallas_call(
        functools.partial(pack_kernel, tiles),
        out_shape=(
            jax.ShapeDtypeStruct((tiles * CHUNK, 4, 128), f32),
            jax.ShapeDtypeStruct((block_count,), i32),
            jax.ShapeDtypeStruct((edge_rows, cells), f32),
            jax.ShapeDtypeStruct((edge_rows, cells), f32),
        ),
        in_specs=[SMEM] + [HBM] * 7,
        out_specs=(HBM, SMEM, HBM, HBM),
        scratch_shapes=[
            pltpu.SMEM((block_count,), i32),
            pltpu.SMEM((block_count,), i32),
            pltpu.SMEM((block_count,), i32),
            pltpu.VMEM((block_count, 4, 128), f32),
            pltpu.VMEM((tiles * CHUNK, 4, 128), f32),
            pltpu.SMEM((tiles,), i32),
            pltpu.VMEM((slots, 128), f32),
            pltpu.VMEM((4, levels, 8, cells), f32),
            pltpu.VMEM((rows, cells), i32),
            pltpu.VMEM((edge_rows, cells), f32),
            pltpu.VMEM((edge_rows, cells), f32),
            pltpu.SemaphoreType.DMA((3,)),
            pltpu.SemaphoreType.DMA((4,)),
            pltpu.SemaphoreType.DMA((4,)),
            pltpu.SemaphoreType.DMA((2,)),
        ],
        compiler_params=whole_grant,
        name="pack",
    )(
        sec, routes.reshape(block_count), dst_block.reshape(block_count),
        weight_index.reshape(block_count), atm_state, depth_levels, ocean_temp, vel_v,
    )

    north_to = [(tiles + t, tiles + t + 1) for t in range(tiles - 1)]
    south_to = [(t + 1, t) for t in range(tiles, 2 * tiles - 1)]
    south = lax.ppermute(up, ("sec", "tile"), north_to)
    north = lax.ppermute(down, ("sec", "tile"), south_to)
    payload, south, north = lax.optimization_barrier((payload, south, north))
    moved = lax.all_to_all(payload, "tile", split_axis=0, concat_axis=0, tiled=True)

    level = lambda count: pl.BlockSpec((1, count, rows, cells), lambda i: (0, 0, 0, 0))
    top = pl.pallas_call(
        functools.partial(surface_kernel, levels),
        grid=(1,),
        out_shape=jax.ShapeDtypeStruct((3, patches, 128), f32),
        in_specs=[
            SMEM,
            level(2),
            level(1),
            level(1),
            pl.BlockSpec((1, rows, cells), lambda i: (0, 0, 0)),
            pl.BlockSpec((edge_rows, cells), lambda i: (0, 0)),
            pl.BlockSpec((edge_rows, cells), lambda i: (0, 0)),
        ],
        out_specs=pl.BlockSpec((3, patches, 128), lambda i: (0, 0, 0)),
        compiler_params=ocean_grant,
        name="surface",
    )(sec, ocean_temp, vel_u, vel_v, depth_levels, south, north)
    top = lax.ppermute(top, "sec", [(1, 0)])

    steps = levels // LEVELS
    slab = pl.BlockSpec((1, LEVELS, rows, cells), lambda i, sec: (0, i * sec[0], 0, 0))
    fixed3 = pl.BlockSpec((1, rows, cells), lambda i, sec: (0, 0, 0))
    fixed2 = pl.BlockSpec((edge_rows, cells), lambda i, sec: (0, 0))
    out = pl.pallas_call(
        functools.partial(ocean_kernel, levels),
        grid_spec=pltpu.PrefetchScalarGridSpec(
            num_scalar_prefetch=1,
            grid=(steps,),
            in_specs=[
                slab,
                pl.BlockSpec(
                    (1, 1, rows, cells),
                    lambda i, sec: (0, jnp.minimum((i + 1) * LEVELS, levels - 1) * sec[0], 0, 0),
                ),
                slab,
                slab,
                fixed3,
                fixed2,
                fixed2,
            ],
            out_specs=pl.BlockSpec((1, LEVELS, rows, cells), lambda i, sec: (0, i, 0, 0)),
            scratch_shapes=[
                pltpu.VMEM((rows, cells), i32),
                pltpu.VMEM((rows, cells), i32),
                pltpu.VMEM((8, cells), i32),
                pltpu.VMEM((rows, cells), f32),
            ],
        ),
        out_shape=jax.ShapeDtypeStruct(ocean_temp.shape, f32),
        compiler_params=ocean_grant,
        cost_estimate=pl.CostEstimate(
            flops=40 * levels * rows * cells,
            bytes_accessed=17 * levels * rows * cells,
            transcendentals=0,
        ),
        name="ocean",
    )(sec, ocean_temp, ocean_temp, vel_u, vel_v, depth_levels, south, north)

    moved, out = lax.optimization_barrier((moved, out))
    ret, fresh = pl.pallas_call(
        functools.partial(heat_kernel, tiles),
        out_shape=(
            jax.ShapeDtypeStruct((slots, 128), f32),
            jax.ShapeDtypeStruct((patches, 128), f32),
        ),
        in_specs=[SMEM, VMEM, VMEM, VMEM],
        out_specs=(VMEM, VMEM),
        scratch_shapes=[pltpu.VMEM((slots, 128), bf16), pltpu.VMEM((slots, 768), bf16)],
        compiler_params=grant,
        name="heat",
    )(sec, moved, top, area_table)

    fresh = lax.ppermute(fresh, "sec", [(0, 1)])
    back = lax.all_to_all(ret, "tile", split_axis=0, concat_axis=0, tiled=True)
    following = pl.pallas_call(
        settle_kernel,
        grid=(1,),
        out_shape=jax.ShapeDtypeStruct(out.shape, f32),
        in_specs=[pl.BlockSpec((patches, 128), lambda i: (0, 0)), ANY],
        out_specs=level(1),
        input_output_aliases={1: 0},
        name="settle",
    )(fresh, out)
    skin = back.at[slot_of].get(mode="promise_in_bounds")
    return following, skin[None]


def solution(mesh):
    return jax.shard_map(
        body,
        mesh=mesh,
        in_specs=(
            P("sec", "tile", None, None),
            P("sec", "tile", None),
            P("sec", "tile"),
            P("sec", "tile"),
            P(),
            P("sec", None, "tile", None),
            P("sec", None, "tile", None),
            P("sec", None, "tile", None),
            P("sec", "tile", None),
        ),
        out_specs=(P("sec", None, "tile", None), P("sec", "tile", None)),
        check_vma=False,
    )
```

```python
import functools

import jax
import jax.numpy as jnp
from jax import lax
from jax.experimental import pallas as pl
from jax.experimental.pallas import tpu as pltpu
from jax.sharding import PartitionSpec as P

HEAT_DIFFUSION = 0.12
VERTICAL_MIXING = 0.2
FLUX_GAIN = 0.5
CAPACITY = 16
CHUNK = CAPACITY + 2
UNROLL = 8
LEVELS = 8

f32, bf16, i32 = jnp.float32, jnp.bfloat16, jnp.int32
VMEM = pl.BlockSpec(memory_space=pltpu.VMEM)
SMEM = pl.BlockSpec(memory_space=pltpu.SMEM)
ANY = pl.BlockSpec(memory_space=pl.ANY)
HBM = pl.BlockSpec(memory_space=pltpu.HBM)


def iota(shape, axis):
    return lax.broadcasted_iota(i32, shape, axis)


def pack_kernel(
    tiles, sec, dest_in, block_in, row_in, state_in, depth_in, temp, merid,
    payload_out, slot_of, up_out, down_out, blank,
    dest, block, row, state, payload, count, entry, edge, depth, up, down,
    nothing, index_sem, state_sem, edge_sem, out_sem, blank_sem,
):
    levels = temp.shape[1]
    rows = temp.shape[2]
    blocks = dest.shape[0]
    pieces = state_sem.shape[0]
    piece = blocks // pieces

    @pl.when(sec[0] == 0)
    def _():
        indices = [
            pltpu.make_async_copy(source, target, index_sem.at[n])
            for n, (source, target) in enumerate(
                ((dest_in, dest), (block_in, block), (row_in, row))
            )
        ]
        states = [
            pltpu.make_async_copy(
                state_in.at[0, pl.ds(n * piece, piece)],
                state.at[pl.ds(n * piece, piece)],
                state_sem.at[n],
            )
            for n in range(pieces)
        ]
        for copy in indices + states:
            copy.start()
        nothing[...] = jnp.zeros_like(nothing)
        blanks = [
            pltpu.make_async_copy(
                nothing, blank.at[0, pl.ds(n * LEVELS, LEVELS)], blank_sem.at[n]
            )
            for n in range(levels // LEVELS)
        ]
        for copy in blanks:
            copy.start()

        for i in range(tiles):
            count[i] = 0
        entry[...] = jnp.full(entry.shape, -1.0, f32)
        is_block = (iota((1, 128), 1) & 32) == 0
        for copy in indices:
            copy.wait()

        def place(step, _):
            for j in range(UNROLL):
                i = step * UNROLL + j
                d = dest[i]
                c = count[d]
                count[d] = c + 1
                c = jnp.minimum(c, CAPACITY - 1)
                slot = d * CAPACITY + c
                slot_of[i] = slot
                payload[d * CHUNK + c] = state[i]
                entry[pl.ds(slot, 1), :] = jnp.where(is_block, block[i], row[i]).astype(f32)
            return 0

        for n in range(pieces):
            states[n].wait()
            lax.fori_loop(n * piece // UNROLL, (n + 1) * piece // UNROLL, place, 0)
        left = iota((8, 128), 1) < 64

        def entries_of(g, _):
            for j in range(8):
                d = g * 8 + j
                low = entry[pl.ds(pl.multiple_of(d * CAPACITY, 8), 8), :]
                high = entry[pl.ds(pl.multiple_of(d * CAPACITY + 8, 8), 8), :]
                both = jnp.where(left, low, high)
                payload[d * CHUNK + CAPACITY] = both[0:4]
                payload[d * CHUNK + CAPACITY + 1] = both[4:8]
            return 0

        lax.fori_loop(0, tiles // 8, entries_of, 0)
        half = payload.shape[0] // 2
        outs = [
            pltpu.make_async_copy(
                payload.at[pl.ds(n * half, half)], payload_out.at[pl.ds(n * half, half)], out_sem.at[n]
            )
            for n in range(2)
        ]
        for copy in outs:
            copy.start()
        for copy in outs + blanks:
            copy.wait()

    @pl.when(sec[0] != 0)
    def _():
        depth_copy = pltpu.make_async_copy(depth_in.at[0], depth, index_sem.at[0])
        depth_copy.start()
        copies = [
            pltpu.make_async_copy(field.at[0, :, pl.ds(lo, 8), :], edge.at[n], edge_sem.at[n])
            for n, (field, lo) in enumerate(
                ((temp, rows - 8), (merid, rows - 8), (temp, 0), (merid, 0))
            )
        ]
        for copy in copies:
            copy.start()

        def none(step, _):
            for j in range(UNROLL):
                slot_of[step * UNROLL + j] = 0
            return 0

        lax.fori_loop(0, blocks // UNROLL, none, 0)
        depth_copy.wait()
        cells = depth.shape[1]
        up[2 * levels :, :] = jnp.broadcast_to(depth[rows - 1 :, :].astype(f32), (8, cells))
        down[2 * levels :, :] = jnp.broadcast_to(depth[0:1, :].astype(f32), (8, cells))
        for n, copy in enumerate(copies):
            copy.wait()
            target = up if n < 2 else down
            target[pl.ds((n % 2) * levels, levels), :] = edge[n, :, 7 if n < 2 else 0, :]
        outs = [
            pltpu.make_async_copy(up, up_out, out_sem.at[0]),
            pltpu.make_async_copy(down, down_out, out_sem.at[1]),
        ]
        for copy in outs:
            copy.start()
        for copy in outs:
            copy.wait()


def faces(k, t, u, v, t_north, v_north, t_s, v_s, depth_e, depth_n, depth_s):
    rows, cells = t.shape
    first = iota((rows, cells), 0) == 0
    last = iota((rows, cells), 0) == rows - 1
    t_e = pltpu.roll(t, cells - 1, 1)
    u_e = pltpu.roll(u, cells - 1, 1)
    east = jnp.where(
        k < depth_e,
        HEAT_DIFFUSION * (t_e - t) - (0.25 * (u + u_e)) * (t + t_e),
        0.0,
    )
    t_n = jnp.where(last, t_north, pltpu.roll(t, rows - 1, 0))
    v_n = jnp.where(last, v_north, pltpu.roll(v, rows - 1, 0))
    northward = jnp.where(
        k < depth_n,
        HEAT_DIFFUSION * (t_n - t) - (0.25 * (v + v_n)) * (t + t_n),
        0.0,
    )
    t_0 = t[0:1]
    southmost = jnp.where(
        k < depth_s,
        HEAT_DIFFUSION * (t_0 - t_s) - (0.25 * (v[0:1] + v_s)) * (t_0 + t_s),
        0.0,
    )
    return (east - pltpu.roll(east, 1, 1)) + (
        northward - jnp.where(first, southmost, pltpu.roll(northward, 1, 0))
    )


def face_depths(d, d_north, d_south):
    rows, cells = d.shape
    last = iota((rows, cells), 0) == rows - 1
    d_north, d_south = d_north.astype(i32), d_south.astype(i32)
    return (
        jnp.minimum(d, pltpu.roll(d, cells - 1, 1)),
        jnp.minimum(d, jnp.where(last, d_north, pltpu.roll(d, rows - 1, 0))),
        jnp.minimum(d[0:1], d_south),
    )


def bring(copies):
    for copy in copies:
        copy.start()
    for copy in copies:
        copy.wait()


def surface_kernel(
    levels, sec, temp, zonal, merid, depth, south, north,
    top,
    t_in, u_in, v_in, d_in, edge, made, sem, out_sem,
):
    @pl.when(sec[0] != 0)
    def _():
        pairs = [
            (temp.at[0, 0:2], t_in),
            (zonal.at[0, 0], u_in),
            (merid.at[0, 0], v_in),
            (depth.at[0], d_in),
        ] + [
            (side.at[pl.ds(n * levels, 8)], edge.at[3 * m + n])
            for m, side in enumerate((north, south))
            for n in range(3)
        ]
        bring([pltpu.make_async_copy(*pair, sem.at[n]) for n, pair in enumerate(pairs)])
        d = d_in[...]
        rows, cells = d.shape
        t = t_in[0]
        row = [edge[n, 0:1, :] for n in range(6)]
        below = jnp.where(1 < d, VERTICAL_MIXING * (t_in[1] - t), 0.0)
        base = t + faces(
            0, t, u_in[...], v_in[...], row[0], row[1], row[3], row[4],
            *face_depths(d, row[2], row[5]),
        ) + below
        wet = jnp.where(d > 0, FLUX_GAIN, 0.0)
        patches = cells // 128
        for p in range(patches):
            part = slice(p * 128, p * 128 + 128)
            made[0, pl.ds(p, rows, stride=patches), :] = t[:, part]
            made[1, pl.ds(p, rows, stride=patches), :] = base[:, part]
            made[2, pl.ds(p, rows, stride=patches), :] = wet[:, part]
        bring([pltpu.make_async_copy(made, top, out_sem)])


def ocean_kernel(
    levels, sec, temp, zonal, merid, depth_in, south_in, north_in, blank,
    out,
    depth, south, north, depth_e, depth_n, depth_s, carry, sem,
):
    rows, cells = depth.shape

    @pl.when(sec[0] != 0)
    def _():
        pairs = [(depth_in.at[0], depth), (south_in, south), (north_in, north)]
        bring([pltpu.make_async_copy(*pair, sem.at[n]) for n, pair in enumerate(pairs)])
        e, n, s = face_depths(
            depth[...], north[2 * levels : 2 * levels + 1, :], south[2 * levels : 2 * levels + 1, :]
        )
        depth_e[...] = e
        depth_n[...] = n
        depth_s[...] = jnp.broadcast_to(s, depth_s.shape)
        carry[...] = jnp.zeros_like(carry)

        def step(index, temp_in, beneath, zonal_in, merid_in, fresh):
            i = index.index[0]
            above = carry[...]
            for j in range(LEVELS):
                k = i * LEVELS + j
                t = temp_in[0, j]
                under = beneath[0, 0] if j == LEVELS - 1 else temp_in[0, j + 1]
                below = jnp.where(k + 1 < depth[...], VERTICAL_MIXING * (under - t), 0.0)
                fresh[0, j] = (
                    t
                    + faces(
                        k, t, zonal_in[0, j], merid_in[0, j],
                        north[pl.ds(k, 1), :], north[pl.ds(levels + k, 1), :],
                        south[pl.ds(k, 1), :], south[pl.ds(levels + k, 1), :],
                        depth_e[...], depth_n[...], depth_s[0:1, :],
                    )
                    + (below - above)
                )
                above = below
            carry[...] = above

        slab = pl.BlockSpec((1, LEVELS, rows, cells), lambda i: (0, i, 0, 0))
        next_level = pl.BlockSpec(
            (1, 1, rows, cells), lambda i: (0, jnp.minimum((i + 1) * LEVELS, levels - 1), 0, 0)
        )
        pltpu.emit_pipeline(
            step,
            grid=(levels // LEVELS,),
            in_specs=[slab, next_level, slab, slab],
            out_specs=[slab],
            _explicit_indices=True,
        )(temp, temp, zonal, merid, out)


def in_three(x):
    high = x.astype(bf16)
    rest = x - high.astype(f32)
    middle = rest.astype(bf16)
    low = (rest - middle.astype(f32)).astype(bf16)
    return jnp.concatenate([high, middle, low], axis=1)


def joined(x, at=0):
    return x[:, at : at + 128] + (x[:, at + 128 : at + 256] + x[:, at + 256 : at + 384])


def heat_kernel(tiles, sec, payload, top, table, ret, fresh, hit, weighted):
    slots = tiles * CAPACITY

    @pl.when(sec[0] != 0)
    def _():
        ret[...] = jnp.zeros_like(ret)
        fresh[...] = jnp.zeros_like(fresh)

    @pl.when(sec[0] == 0)
    def _():
        surface_parts = in_three(top[0])
        table_parts = in_three(
            jnp.concatenate([table[...], jnp.zeros((128 - table.shape[0], 128), f32)], axis=0)
        )
        lane = iota((1, 8, 128), 2).astype(f32)
        group = 8

        def step(g, _):
            base = pl.multiple_of(g * group, group)
            upper = payload[pl.ds(base * CHUNK, group * CHUNK)].reshape(group, CHUNK, 4, 128)
            entry = upper[:, CAPACITY:].reshape(group, 8, 128)
            at = pl.multiple_of(base * CAPACITY, group * CAPACITY)
            size = group * CAPACITY
            block_hit = jnp.concatenate(
                [entry[:, None, :, 0:1] == lane[None], entry[:, None, :, 64:65] == lane[None]],
                axis=1,
            ).reshape(size, 128)
            row_hit = jnp.concatenate(
                [entry[:, None, :, 32:33] == lane[None], entry[:, None, :, 96:97] == lane[None]],
                axis=1,
            ).reshape(size, 128)
            live = jnp.concatenate(
                [
                    jnp.broadcast_to(entry[:, None, :, 0:1], (group, 1, 8, 128)),
                    jnp.broadcast_to(entry[:, None, :, 64:65], (group, 1, 8, 128)),
                ],
                axis=1,
            ).reshape(size, 128) >= 0
            block_one = jnp.where(block_hit, 1.0, 0.0).astype(bf16)
            row_one = jnp.where(row_hit, 1.0, 0.0).astype(bf16)
            hit[pl.ds(at, size), :] = block_one
            surface = joined(jnp.dot(block_one, surface_parts, preferred_element_type=f32))
            weights = joined(jnp.dot(row_one, table_parts, preferred_element_type=f32))

            def channel(c):
                return upper[:, :CAPACITY, c, :].reshape(size, 128)

            contrast = surface - channel(1)
            transfer = 0.8 + 0.4 * jnp.tanh(contrast)
            saturation = 0.6 * jnp.exp(0.3 * surface)
            heat = channel(3) - transfer * channel(0) * (
                contrast + 1.5 * (saturation - channel(2))
            )
            product = jnp.where(live, weights * heat, 0.0)
            weighted[pl.ds(at, size), 0:384] = in_three(product)
            weighted[pl.ds(at, size), 384:768] = in_three(weights)
            return 0

        lax.fori_loop(0, tiles // group, step, 0)
        sums = lax.dot_general(
            hit[...], weighted[...], (((0,), (0,)), ((), ())), preferred_element_type=f32
        )
        forcing = joined(sums) / jnp.maximum(joined(sums, 384), 1.0)
        new_top = top[1] + top[2] * forcing
        fresh[...] = new_top
        ret[...] = joined(jnp.dot(hit[...], in_three(new_top), preferred_element_type=f32))


def settle_kernel(sec, fresh, whole, out, level, sem):
    @pl.when(sec[0] != 0)
    def _():
        rows, cells = level.shape
        patches = cells // 128
        for p in range(patches):
            level[:, p * 128 : p * 128 + 128] = fresh[pl.ds(p, rows, stride=patches), :]
        bring([pltpu.make_async_copy(level, out.at[0, 0], sem)])


def body(
    atm_state, routes, dst_block, weight_index, area_table, ocean_temp, vel_u, vel_v, depth_levels
):
    tiles = lax.axis_size("tile")
    block_count = atm_state.shape[1]
    levels, rows, cells = ocean_temp.shape[1:]
    patches = rows * cells // 128
    slots = tiles * CAPACITY
    sec = lax.axis_index("sec").astype(i32).reshape(1)
    grant = pltpu.CompilerParams(vmem_limit_bytes=24 << 20)
    ocean_grant = pltpu.CompilerParams(vmem_limit_bytes=56 << 20)
    whole_grant = pltpu.CompilerParams(vmem_limit_bytes=60 << 20)

    edge_rows = 2 * levels + 8
    payload, slot_of, up, down, blank = pl.pallas_call(
        functools.partial(pack_kernel, tiles),
        out_shape=(
            jax.ShapeDtypeStruct((tiles * CHUNK, 4, 128), f32),
            jax.ShapeDtypeStruct((block_count,), i32),
            jax.ShapeDtypeStruct((edge_rows, cells), f32),
            jax.ShapeDtypeStruct((edge_rows, cells), f32),
            jax.ShapeDtypeStruct(ocean_temp.shape, f32),
        ),
        in_specs=[SMEM] + [HBM] * 7,
        out_specs=(HBM, SMEM, HBM, HBM, HBM),
        scratch_shapes=[
            pltpu.SMEM((block_count,), i32),
            pltpu.SMEM((block_count,), i32),
            pltpu.SMEM((block_count,), i32),
            pltpu.VMEM((block_count, 4, 128), f32),
            pltpu.VMEM((tiles * CHUNK, 4, 128), f32),
            pltpu.SMEM((tiles,), i32),
            pltpu.VMEM((slots, 128), f32),
            pltpu.VMEM((4, levels, 8, cells), f32),
            pltpu.VMEM((rows, cells), i32),
            pltpu.VMEM((edge_rows, cells), f32),
            pltpu.VMEM((edge_rows, cells), f32),
            pltpu.VMEM((LEVELS, rows, cells), f32),
            pltpu.SemaphoreType.DMA((3,)),
            pltpu.SemaphoreType.DMA((4,)),
            pltpu.SemaphoreType.DMA((4,)),
            pltpu.SemaphoreType.DMA((2,)),
            pltpu.SemaphoreType.DMA((levels // LEVELS,)),
        ],
        compiler_params=whole_grant,
        name="pack",
    )(
        sec, routes.reshape(block_count), dst_block.reshape(block_count),
        weight_index.reshape(block_count), atm_state, depth_levels, ocean_temp, vel_v,
    )

    def among_atmosphere(value):
        return lax.cond(
            sec[0] == 0,
            lambda v: lax.all_to_all(v, "tile", split_axis=0, concat_axis=0, tiled=True),
            lambda v: v,
            value,
        )

    north_to = [(tiles + t, tiles + t + 1) for t in range(tiles - 1)]
    south_to = [(t + 1, t) for t in range(tiles, 2 * tiles - 1)]
    south = lax.ppermute(up, ("sec", "tile"), north_to)
    north = lax.ppermute(down, ("sec", "tile"), south_to)
    top = pl.pallas_call(
        functools.partial(surface_kernel, levels),
        out_shape=jax.ShapeDtypeStruct((3, patches, 128), f32),
        in_specs=[SMEM] + [HBM] * 6,
        out_specs=HBM,
        scratch_shapes=[
            pltpu.VMEM((2, rows, cells), f32),
            pltpu.VMEM((rows, cells), f32),
            pltpu.VMEM((rows, cells), f32),
            pltpu.VMEM((rows, cells), i32),
            pltpu.VMEM((6, 8, cells), f32),
            pltpu.VMEM((3, patches, 128), f32),
            pltpu.SemaphoreType.DMA((10,)),
            pltpu.SemaphoreType.DMA(()),
        ],
        compiler_params=ocean_grant,
        name="surface",
    )(sec, ocean_temp, vel_u, vel_v, depth_levels, south, north)
    payload, top = lax.optimization_barrier((payload, top))
    top = lax.ppermute(top, "sec", [(1, 0)])
    moved = among_atmosphere(payload)

    moved, south, north = lax.optimization_barrier((moved, south, north))
    out = pl.pallas_call(
        functools.partial(ocean_kernel, levels),
        in_specs=[SMEM] + [HBM] * 7,
        out_specs=HBM,
        out_shape=jax.ShapeDtypeStruct(ocean_temp.shape, f32),
        scratch_shapes=[
            pltpu.VMEM((rows, cells), i32),
            pltpu.VMEM((edge_rows, cells), f32),
            pltpu.VMEM((edge_rows, cells), f32),
            pltpu.VMEM((rows, cells), i32),
            pltpu.VMEM((rows, cells), i32),
            pltpu.VMEM((8, cells), i32),
            pltpu.VMEM((rows, cells), f32),
            pltpu.SemaphoreType.DMA((3,)),
        ],
        input_output_aliases={7: 0},
        compiler_params=ocean_grant,
        cost_estimate=pl.CostEstimate(
            flops=40 * levels * rows * cells,
            bytes_accessed=17 * levels * rows * cells,
            transcendentals=0,
        ),
        name="ocean",
    )(sec, ocean_temp, vel_u, vel_v, depth_levels, south, north, blank)

    ret, fresh = pl.pallas_call(
        functools.partial(heat_kernel, tiles),
        out_shape=(
            jax.ShapeDtypeStruct((slots, 128), f32),
            jax.ShapeDtypeStruct((patches, 128), f32),
        ),
        in_specs=[SMEM, VMEM, VMEM, VMEM],
        out_specs=(VMEM, VMEM),
        scratch_shapes=[pltpu.VMEM((slots, 128), bf16), pltpu.VMEM((slots, 768), bf16)],
        compiler_params=grant,
        name="heat",
    )(sec, moved, top, area_table)

    fresh = lax.ppermute(fresh, "sec", [(0, 1)])
    back = among_atmosphere(ret)
    following = pl.pallas_call(
        settle_kernel,
        out_shape=jax.ShapeDtypeStruct(out.shape, f32),
        in_specs=[SMEM, VMEM, HBM],
        out_specs=HBM,
        scratch_shapes=[pltpu.VMEM((rows, cells), f32), pltpu.SemaphoreType.DMA(())],
        input_output_aliases={2: 0},
        name="settle",
    )(sec, fresh, out)
    skin = back.at[slot_of].get(mode="promise_in_bounds")
    return following, skin[None]


def solution(mesh):
    return jax.shard_map(
        body,
        mesh=mesh,
        in_specs=(
            P("sec", "tile", None, None),
            P("sec", "tile", None),
            P("sec", "tile"),
            P("sec", "tile"),
            P(),
            P("sec", None, "tile", None),
            P("sec", None, "tile", None),
            P("sec", None, "tile", None),
            P("sec", "tile", None),
        ),
        out_specs=(P("sec", None, "tile", None), P("sec", "tile", None)),
        check_vma=False,
    )
```

```python
import functools

import jax
import jax.numpy as jnp
from jax import lax
from jax.experimental import pallas as pl
from jax.experimental.pallas import tpu as pltpu
from jax.sharding import PartitionSpec as P

HEAT_DIFFUSION = 0.12
VERTICAL_MIXING = 0.2
FLUX_GAIN = 0.5
CAPACITY = 16
CHUNK = CAPACITY + 2
UNROLL = 8
LEVELS = 8

f32, bf16, i32 = jnp.float32, jnp.bfloat16, jnp.int32
VMEM = pl.BlockSpec(memory_space=pltpu.VMEM)
SMEM = pl.BlockSpec(memory_space=pltpu.SMEM)
ANY = pl.BlockSpec(memory_space=pl.ANY)
HBM = pl.BlockSpec(memory_space=pltpu.HBM)


def iota(shape, axis):
    return lax.broadcasted_iota(i32, shape, axis)


def pack_kernel(
    tiles, sec, dest_in, block_in, row_in, state_in, depth_in, temp, merid,
    payload, slot_of, up, down, brief_up, brief_down, blank,
    dest, block, row, state, count, entry, edge, depth,
    nothing, index_sem, state_sem, edge_sem, blank_sem,
):
    levels = temp.shape[1]
    rows = temp.shape[2]
    blocks = dest.shape[0]
    pieces = state_sem.shape[0]
    piece = blocks // pieces

    @pl.when(sec[0] == 0)
    def _():
        indices = [
            pltpu.make_async_copy(source, target, index_sem.at[n])
            for n, (source, target) in enumerate(
                ((dest_in, dest), (block_in, block), (row_in, row))
            )
        ]
        states = [
            pltpu.make_async_copy(
                state_in.at[0, pl.ds(n * piece, piece)],
                state.at[pl.ds(n * piece, piece)],
                state_sem.at[n],
            )
            for n in range(pieces)
        ]
        for copy in indices + states:
            copy.start()
        nothing[...] = jnp.zeros_like(nothing)
        blanks = [
            pltpu.make_async_copy(
                nothing, blank.at[0, pl.ds(n * LEVELS, LEVELS)], blank_sem.at[n]
            )
            for n in range(levels // LEVELS)
        ]
        for copy in blanks:
            copy.start()

        for i in range(tiles):
            count[i] = 0
        entry[...] = jnp.full(entry.shape, -1.0, f32)
        is_block = (iota((1, 128), 1) & 32) == 0
        for copy in indices:
            copy.wait()

        def place(step, _):
            for j in range(UNROLL):
                i = step * UNROLL + j
                d = dest[i]
                c = count[d]
                count[d] = c + 1
                c = jnp.minimum(c, CAPACITY - 1)
                slot = d * CAPACITY + c
                slot_of[i] = slot
                payload[d * CHUNK + c] = state[i]
                entry[pl.ds(slot, 1), :] = jnp.where(is_block, block[i], row[i]).astype(f32)
            return 0

        for n in range(pieces):
            states[n].wait()
            lax.fori_loop(n * piece // UNROLL, (n + 1) * piece // UNROLL, place, 0)
        left = iota((8, 128), 1) < 64

        def entries_of(g, _):
            for j in range(8):
                d = g * 8 + j
                low = entry[pl.ds(pl.multiple_of(d * CAPACITY, 8), 8), :]
                high = entry[pl.ds(pl.multiple_of(d * CAPACITY + 8, 8), 8), :]
                both = jnp.where(left, low, high)
                payload[d * CHUNK + CAPACITY] = both[0:4]
                payload[d * CHUNK + CAPACITY + 1] = both[4:8]
            return 0

        lax.fori_loop(0, tiles // 8, entries_of, 0)
        for copy in blanks:
            copy.wait()

    @pl.when(sec[0] != 0)
    def _():
        depth_copy = pltpu.make_async_copy(depth_in.at[0], depth, index_sem.at[0])
        depth_copy.start()
        copies = [
            pltpu.make_async_copy(field.at[0, :, pl.ds(lo, 8), :], edge.at[n], edge_sem.at[n])
            for n, (field, lo) in enumerate(
                ((temp, rows - 8), (merid, rows - 8), (temp, 0), (merid, 0))
            )
        ]
        for copy in copies:
            copy.start()

        def none(step, _):
            for j in range(UNROLL):
                slot_of[step * UNROLL + j] = 0
            return 0

        lax.fori_loop(0, blocks // UNROLL, none, 0)
        depth_copy.wait()
        for side, line in ((up, rows - 1), (down, 0)):
            side[2 * levels :, :] = jnp.broadcast_to(
                depth[line : line + 1, :].astype(f32), (8, depth.shape[1])
            )
        for n, copy in enumerate(copies):
            copy.wait()
            side = up if n < 2 else down
            side[pl.ds((n % 2) * levels, levels), :] = edge[n, :, 7 if n < 2 else 0, :]
        for side, brief in ((up, brief_up), (down, brief_down)):
            for m in range(3):
                brief[m : m + 1, :] = side[m * levels : m * levels + 1, :]


def through(k, depth, t, t_next, speed, speed_next):
    return jnp.where(
        k < depth,
        HEAT_DIFFUSION * (t_next - t) - (0.25 * (speed + speed_next)) * (t + t_next),
        0.0,
    )


def inner_faces(k, t, u, v, depth_e, depth_n):
    rows, cells = t.shape
    first = iota((rows, cells), 0) == 0
    east = through(k, depth_e, t, pltpu.roll(t, cells - 1, 1), u, pltpu.roll(u, cells - 1, 1))
    north = through(k, depth_n, t, pltpu.roll(t, rows - 1, 0), v, pltpu.roll(v, rows - 1, 0))
    return (east - pltpu.roll(east, 1, 1)) + (
        north - jnp.where(first, 0.0, pltpu.roll(north, 1, 0))
    )


def inner_depths(d):
    rows, cells = d.shape
    last = iota((rows, cells), 0) == rows - 1
    return (
        jnp.minimum(d, pltpu.roll(d, cells - 1, 1)),
        jnp.where(last, 0, jnp.minimum(d, pltpu.roll(d, rows - 1, 0))),
    )


def bring(copies):
    for copy in copies:
        copy.start()
    for copy in copies:
        copy.wait()


def surface_kernel(
    sec, temp, zonal, merid, depth, south, north,
    top,
    t_in, u_in, v_in, d_in, edge, made, sem, out_sem,
):
    @pl.when(sec[0] != 0)
    def _():
        pairs = [
            (temp.at[0, 0:2], t_in),
            (zonal.at[0, 0], u_in),
            (merid.at[0, 0], v_in),
            (depth.at[0], d_in),
            (north, edge.at[0]),
            (south, edge.at[1]),
        ]
        bring([pltpu.make_async_copy(*pair, sem.at[n]) for n, pair in enumerate(pairs)])
        d = d_in[...]
        rows, cells = d.shape
        t, v = t_in[0], v_in[...]
        t_n, v_n, d_n = (edge[0, m : m + 1, :] for m in range(3))
        t_s, v_s, d_s = (edge[1, m : m + 1, :] for m in range(3))
        end = slice(rows - 1, rows)
        northmost = through(
            0, jnp.minimum(d[end], d_n.astype(i32)), t[end], t_n, v[end], v_n
        )
        southmost = through(0, jnp.minimum(d[0:1], d_s.astype(i32)), t_s, t[0:1], v_s, v[0:1])
        at = iota((rows, cells), 0)
        outer = jnp.where(at == rows - 1, northmost, 0.0) - jnp.where(at == 0, southmost, 0.0)
        below = jnp.where(1 < d, VERTICAL_MIXING * (t_in[1] - t), 0.0)
        base = t + (inner_faces(0, t, u_in[...], v, *inner_depths(d)) + outer) + below
        wet = jnp.where(d > 0, FLUX_GAIN, 0.0)
        patches = cells // 128
        for p in range(patches):
            part = slice(p * 128, p * 128 + 128)
            made[0, pl.ds(p, rows, stride=patches), :] = t[:, part]
            made[1, pl.ds(p, rows, stride=patches), :] = base[:, part]
            made[2, pl.ds(p, rows, stride=patches), :] = wet[:, part]
        bring([pltpu.make_async_copy(made, top, out_sem)])


def ocean_kernel(
    levels, temp, zonal, merid, depth_in,
    out,
    depth, depth_e, depth_n, carry, sem,
):
    rows, cells = depth.shape
    bring([pltpu.make_async_copy(depth_in.at[0], depth, sem)])
    e, n = inner_depths(depth[...])
    depth_e[...] = e
    depth_n[...] = n
    carry[...] = jnp.zeros_like(carry)

    def step(index, temp_in, beneath, zonal_in, merid_in, fresh):
        i = index.index[0]
        above = carry[...]
        for j in range(LEVELS):
            k = i * LEVELS + j
            t = temp_in[0, j]
            under = beneath[0, 0] if j == LEVELS - 1 else temp_in[0, j + 1]
            below = jnp.where(k + 1 < depth[...], VERTICAL_MIXING * (under - t), 0.0)
            inner = inner_faces(k, t, zonal_in[0, j], merid_in[0, j], depth_e[...], depth_n[...])
            fresh[0, j] = t + inner + (below - above)
            above = below
        carry[...] = above

    slab = pl.BlockSpec((1, LEVELS, rows, cells), lambda i: (0, i, 0, 0))
    next_level = pl.BlockSpec(
        (1, 1, rows, cells), lambda i: (0, jnp.minimum((i + 1) * LEVELS, levels - 1), 0, 0)
    )
    pltpu.emit_pipeline(
        step,
        grid=(levels // LEVELS,),
        in_specs=[slab, next_level, slab, slab],
        out_specs=[slab],
        _explicit_indices=True,
    )(temp, temp, zonal, merid, out)


def settle_kernel(
    levels, sec, up_in, down_in, south_in, north_in, fresh_in, middle, blank,
    out,
    up, down, south, north, fresh, field, northmost, southmost, side_sem, in_sem, out_sem,
):
    rows, cells = field.shape[1:]
    patches = cells // 128

    @pl.when(sec[0] != 0)
    def _():
        pairs = (
            (up_in, up), (down_in, down), (south_in, south), (north_in, north), (fresh_in, fresh)
        )
        sides = [pltpu.make_async_copy(*pair, side_sem.at[n]) for n, pair in enumerate(pairs)]
        parts = [pl.ds(n * LEVELS, LEVELS) for n in range(levels // LEVELS)]
        ins = [
            pltpu.make_async_copy(middle.at[0, part], field.at[part], in_sem.at[n])
            for n, part in enumerate(parts)
        ]
        outs = [
            pltpu.make_async_copy(field.at[part], out.at[0, part], out_sem.at[n])
            for n, part in enumerate(parts)
        ]
        for copy in sides + ins:
            copy.start()
        for copy in sides:
            copy.wait()
        own_n = up[2 * levels : 2 * levels + 1, :].astype(i32)
        own_s = down[2 * levels : 2 * levels + 1, :].astype(i32)
        d_n = jnp.minimum(own_n, north[2 * levels : 2 * levels + 1, :].astype(i32))
        d_s = jnp.minimum(own_s, south[2 * levels : 2 * levels + 1, :].astype(i32))
        for at in range(0, levels, 8):
            k = iota((8, cells), 0) + at
            t, v = slice(at, at + 8), slice(levels + at, levels + at + 8)
            northmost[t, :] = through(k, d_n, up[t, :], north[t, :], up[v, :], north[v, :])
            southmost[t, :] = through(k, d_s, south[t, :], down[t, :], south[v, :], down[v, :])
        for n in range(len(parts)):
            ins[n].wait()
            for k in range(n * LEVELS, (n + 1) * LEVELS):
                field[k, rows - 1 : rows, :] += northmost[k : k + 1, :]
                field[k, 0:1, :] -= southmost[k : k + 1, :]
            if n == 0:
                for p in range(patches):
                    field[0, :, p * 128 : p * 128 + 128] = fresh[pl.ds(p, rows, stride=patches), :]
            outs[n].start()
        for copy in outs:
            copy.wait()


def in_three(x):
    high = x.astype(bf16)
    rest = x - high.astype(f32)
    middle = rest.astype(bf16)
    low = (rest - middle.astype(f32)).astype(bf16)
    return jnp.concatenate([high, middle, low], axis=1)


def joined(x, at=0):
    return x[:, at : at + 128] + (x[:, at + 128 : at + 256] + x[:, at + 256 : at + 384])


def heat_kernel(tiles, sec, payload, top, table, ret, fresh, hit, weighted):
    slots = tiles * CAPACITY

    @pl.when(sec[0] != 0)
    def _():
        ret[...] = jnp.zeros_like(ret)
        fresh[...] = jnp.zeros_like(fresh)

    @pl.when(sec[0] == 0)
    def _():
        surface_parts = in_three(top[0])
        table_parts = in_three(
            jnp.concatenate([table[...], jnp.zeros((128 - table.shape[0], 128), f32)], axis=0)
        )
        lane = iota((1, 8, 128), 2).astype(f32)
        group = min(16, tiles)

        def step(g, _):
            base = pl.multiple_of(g * group, group)
            upper = payload[pl.ds(base * CHUNK, group * CHUNK)].reshape(group, CHUNK, 4, 128)
            entry = upper[:, CAPACITY:].reshape(group, 8, 128)
            at = pl.multiple_of(base * CAPACITY, group * CAPACITY)
            size = group * CAPACITY
            block_hit = jnp.concatenate(
                [entry[:, None, :, 0:1] == lane[None], entry[:, None, :, 64:65] == lane[None]],
                axis=1,
            ).reshape(size, 128)
            row_hit = jnp.concatenate(
                [entry[:, None, :, 32:33] == lane[None], entry[:, None, :, 96:97] == lane[None]],
                axis=1,
            ).reshape(size, 128)
            live = jnp.concatenate(
                [
                    jnp.broadcast_to(entry[:, None, :, 0:1], (group, 1, 8, 128)),
                    jnp.broadcast_to(entry[:, None, :, 64:65], (group, 1, 8, 128)),
                ],
                axis=1,
            ).reshape(size, 128) >= 0
            block_one = jnp.where(block_hit, 1.0, 0.0).astype(bf16)
            row_one = jnp.where(row_hit, 1.0, 0.0).astype(bf16)
            hit[pl.ds(at, size), :] = block_one
            surface = joined(jnp.dot(block_one, surface_parts, preferred_element_type=f32))
            weights = joined(jnp.dot(row_one, table_parts, preferred_element_type=f32))

            def channel(c):
                return upper[:, :CAPACITY, c, :].reshape(size, 128)

            contrast = surface - channel(1)
            transfer = 0.8 + 0.4 * jnp.tanh(contrast)
            saturation = 0.6 * jnp.exp(0.3 * surface)
            heat = channel(3) - transfer * channel(0) * (
                contrast + 1.5 * (saturation - channel(2))
            )
            product = jnp.where(live, weights * heat, 0.0)
            weighted[pl.ds(at, size), 0:384] = in_three(product)
            weighted[pl.ds(at, size), 384:768] = in_three(weights)
            return 0

        lax.fori_loop(0, tiles // group, step, 0)
        sums = lax.dot_general(
            hit[...], weighted[...], (((0,), (0,)), ((), ())), preferred_element_type=f32
        )
        forcing = joined(sums) / jnp.maximum(joined(sums, 384), 1.0)
        new_top = top[1] + top[2] * forcing
        fresh[...] = new_top
        ret[...] = joined(jnp.dot(hit[...], in_three(new_top), preferred_element_type=f32))


def nothing_kernel(*refs):
    pass


def body(
    atm_state, routes, dst_block, weight_index, area_table, ocean_temp, vel_u, vel_v, depth_levels
):
    tiles = lax.axis_size("tile")
    block_count = atm_state.shape[1]
    levels, rows, cells = ocean_temp.shape[1:]
    patches = rows * cells // 128
    slots = tiles * CAPACITY
    sec = lax.axis_index("sec").astype(i32).reshape(1)
    grant = pltpu.CompilerParams(vmem_limit_bytes=24 << 20)
    ocean_grant = pltpu.CompilerParams(vmem_limit_bytes=56 << 20)
    whole_grant = pltpu.CompilerParams(vmem_limit_bytes=60 << 20)

    edge_rows = 2 * levels + 8
    payload, slot_of, up, down, brief_up, brief_down, blank = pl.pallas_call(
        functools.partial(pack_kernel, tiles),
        out_shape=(
            jax.ShapeDtypeStruct((tiles * CHUNK, 4, 128), f32),
            jax.ShapeDtypeStruct((block_count,), i32),
            jax.ShapeDtypeStruct((edge_rows, cells), f32),
            jax.ShapeDtypeStruct((edge_rows, cells), f32),
            jax.ShapeDtypeStruct((8, cells), f32),
            jax.ShapeDtypeStruct((8, cells), f32),
            jax.ShapeDtypeStruct(ocean_temp.shape, f32),
        ),
        in_specs=[SMEM] + [HBM] * 7,
        out_specs=(VMEM, SMEM, VMEM, VMEM, VMEM, VMEM, HBM),
        scratch_shapes=[
            pltpu.SMEM((block_count,), i32),
            pltpu.SMEM((block_count,), i32),
            pltpu.SMEM((block_count,), i32),
            pltpu.VMEM((block_count, 4, 128), f32),
            pltpu.SMEM((tiles,), i32),
            pltpu.VMEM((slots, 128), f32),
            pltpu.VMEM((4, levels, 8, cells), f32),
            pltpu.VMEM((rows, cells), i32),
            pltpu.VMEM((LEVELS, rows, cells), f32),
            pltpu.SemaphoreType.DMA((3,)),
            pltpu.SemaphoreType.DMA((4,)),
            pltpu.SemaphoreType.DMA((4,)),
            pltpu.SemaphoreType.DMA((levels // LEVELS,)),
        ],
        compiler_params=whole_grant,
        name="pack",
    )(
        sec, routes.reshape(block_count), dst_block.reshape(block_count),
        weight_index.reshape(block_count), atm_state, depth_levels, ocean_temp, vel_v,
    )

    def unwritten(shapes):
        return pl.pallas_call(
            nothing_kernel,
            out_shape=shapes,
            out_specs=tuple(HBM for _ in shapes),
            compiler_params=ocean_grant,
            name="nothing",
        )()

    def from_sides(northmost, southmost):
        north_to = [(tiles + t, tiles + t + 1) for t in range(tiles - 1)]
        south_to = [(t + 1, t) for t in range(tiles, 2 * tiles - 1)]
        return (
            lax.ppermute(northmost, ("sec", "tile"), north_to),
            lax.ppermute(southmost, ("sec", "tile"), south_to),
        )

    top_shape = jax.ShapeDtypeStruct((3, patches, 128), f32)
    edge_shape = jax.ShapeDtypeStruct((edge_rows, cells), f32)
    field_shape = jax.ShapeDtypeStruct(ocean_temp.shape, f32)

    def split(atmosphere, ocean, *values):
        return lax.cond(sec[0] == 0, atmosphere, ocean, *values)

    def exchanged(value):
        return lax.all_to_all(value, "tile", split_axis=0, concat_axis=0, tiled=True)

    def surface(brief_up, brief_down):
        south, north = from_sides(brief_up, brief_down)
        return pl.pallas_call(
            surface_kernel,
            out_shape=top_shape,
            in_specs=[SMEM] + [HBM] * 4 + [ANY] * 2,
            out_specs=HBM,
            scratch_shapes=[
                pltpu.VMEM((2, rows, cells), f32),
                pltpu.VMEM((rows, cells), f32),
                pltpu.VMEM((rows, cells), f32),
                pltpu.VMEM((rows, cells), i32),
                pltpu.VMEM((2, 8, cells), f32),
                pltpu.VMEM((3, patches, 128), f32),
                pltpu.SemaphoreType.DMA((6,)),
                pltpu.SemaphoreType.DMA(()),
            ],
            compiler_params=ocean_grant,
            name="surface",
        )(sec, ocean_temp, vel_u, vel_v, depth_levels, south, north)

    def middle_of(temp, zonal, merid, depth):
        return pl.pallas_call(
            functools.partial(ocean_kernel, levels),
            in_specs=[HBM] * 4,
            out_specs=HBM,
            out_shape=field_shape,
            scratch_shapes=[
                pltpu.VMEM((rows, cells), i32),
                pltpu.VMEM((rows, cells), i32),
                pltpu.VMEM((rows, cells), i32),
                pltpu.VMEM((rows, cells), f32),
                pltpu.SemaphoreType.DMA(()),
            ],
            compiler_params=ocean_grant,
            name="ocean",
        )(temp, zonal, merid, depth)

    top = split(
        lambda up, down: unwritten((top_shape,))[0], surface, brief_up, brief_down
    )
    payload, up, down, top = lax.optimization_barrier((payload, up, down, top))
    top = lax.ppermute(top, "sec", [(1, 0)])

    def first_atmosphere(payload):
        payload, middle = lax.optimization_barrier((payload, unwritten((field_shape,))[0]))
        return exchanged(payload), middle

    moved, middle = split(
        first_atmosphere,
        lambda payload: (payload, middle_of(ocean_temp, vel_u, vel_v, depth_levels)),
        payload,
    )

    ret, fresh = pl.pallas_call(
        functools.partial(heat_kernel, tiles),
        out_shape=(
            jax.ShapeDtypeStruct((slots, 128), f32),
            jax.ShapeDtypeStruct((patches, 128), f32),
        ),
        in_specs=[SMEM, VMEM, VMEM, VMEM],
        out_specs=(VMEM, VMEM),
        scratch_shapes=[pltpu.VMEM((slots, 128), bf16), pltpu.VMEM((slots, 768), bf16)],
        compiler_params=grant,
        name="heat",
    )(sec, moved, top, area_table)
    fresh = lax.ppermute(fresh, "sec", [(0, 1)])

    def second_atmosphere(ret, up, down):
        ret, south, north = lax.optimization_barrier((ret, *unwritten((edge_shape, edge_shape))))
        return exchanged(ret), south, north

    back, south, north = split(
        second_atmosphere, lambda ret, up, down: (ret, *from_sides(up, down)), ret, up, down
    )
    skin = back.at[slot_of].get(mode="promise_in_bounds")
    following = pl.pallas_call(
        functools.partial(settle_kernel, levels),
        out_shape=field_shape,
        in_specs=[SMEM] + [ANY] * 5 + [HBM] * 2,
        out_specs=HBM,
        scratch_shapes=[pltpu.VMEM((edge_rows, cells), f32)] * 4
        + [
            pltpu.VMEM((patches, 128), f32),
            pltpu.VMEM((levels, rows, cells), f32),
            pltpu.VMEM((levels, cells), f32),
            pltpu.VMEM((levels, cells), f32),
            pltpu.SemaphoreType.DMA((5,)),
            pltpu.SemaphoreType.DMA((levels // LEVELS,)),
            pltpu.SemaphoreType.DMA((levels // LEVELS,)),
        ],
        input_output_aliases={7: 0},
        compiler_params=grant,
        name="settle",
    )(sec, up, down, south, north, fresh, middle, blank)
    return following, skin[None]


def solution(mesh):
    return jax.shard_map(
        body,
        mesh=mesh,
        in_specs=(
            P("sec", "tile", None, None),
            P("sec", "tile", None),
            P("sec", "tile"),
            P("sec", "tile"),
            P(),
            P("sec", None, "tile", None),
            P("sec", None, "tile", None),
            P("sec", None, "tile", None),
            P("sec", "tile", None),
        ),
        out_specs=(P("sec", None, "tile", None), P("sec", "tile", None)),
        check_vma=False,
    )
```

```python
import functools

import jax
import jax.numpy as jnp
from jax import lax
from jax.experimental import pallas as pl
from jax.experimental.pallas import tpu as pltpu
from jax.sharding import PartitionSpec as P

HEAT_DIFFUSION = 0.12
VERTICAL_MIXING = 0.2
FLUX_GAIN = 0.5
CAPACITY = 16
CHUNK = CAPACITY + 2
UNROLL = 8
LEVELS = 16

f32, bf16, i32 = jnp.float32, jnp.bfloat16, jnp.int32
VMEM = pl.BlockSpec(memory_space=pltpu.VMEM)
SMEM = pl.BlockSpec(memory_space=pltpu.SMEM)
ANY = pl.BlockSpec(memory_space=pl.ANY)
HBM = pl.BlockSpec(memory_space=pltpu.HBM)


def iota(shape, axis):
    return lax.broadcasted_iota(i32, shape, axis)


def pack_kernel(
    tiles, sec, dest_in, block_in, row_in, state_in, depth_in, temp, merid,
    payload, slot_of, up, down, brief_up, brief_down, blank,
    dest, block, row, state, count, entry, edge, depth,
    nothing, index_sem, state_sem, edge_sem, blank_sem,
):
    levels = temp.shape[1]
    rows = temp.shape[2]
    blocks = dest.shape[0]
    pieces = state_sem.shape[0]
    piece = blocks // pieces

    @pl.when(sec[0] == 0)
    def _():
        indices = [
            pltpu.make_async_copy(source, target, index_sem.at[n])
            for n, (source, target) in enumerate(
                ((dest_in, dest), (block_in, block), (row_in, row))
            )
        ]
        states = [
            pltpu.make_async_copy(
                state_in.at[0, pl.ds(n * piece, piece)],
                state.at[pl.ds(n * piece, piece)],
                state_sem.at[n],
            )
            for n in range(pieces)
        ]
        for copy in indices + states:
            copy.start()
        nothing[...] = jnp.zeros_like(nothing)
        blanks = [
            pltpu.make_async_copy(
                nothing, blank.at[0, pl.ds(n * LEVELS, LEVELS)], blank_sem.at[n]
            )
            for n in range(levels // LEVELS)
        ]
        for copy in blanks:
            copy.start()

        for i in range(tiles):
            count[i] = i * CHUNK
        entry[...] = jnp.full(entry.shape, -1, i32)
        is_block = (iota((1, 128), 1) & 32) == 0
        for copy in indices:
            copy.wait()

        def place(step, _):
            for j in range(UNROLL):
                i = step * UNROLL + j
                d = dest[i]
                place_of = count[d]
                count[d] = place_of + 1
                slot_of[i] = place_of
                payload[place_of] = state[i]
                entry[pl.ds(place_of, 1), :] = jnp.where(is_block, block[i], row[i])
            return 0

        for n in range(pieces):
            states[n].wait()
            lax.fori_loop(n * piece // UNROLL, (n + 1) * piece // UNROLL, place, 0)
        left = iota((8, 128), 1) < 64

        def entries_of(g, _):
            for j in range(8):
                d = g * 8 + j
                low = entry[pl.ds(d * CHUNK, 8), :]
                high = entry[pl.ds(d * CHUNK + 8, 8), :]
                both = jnp.where(left, low, high).astype(f32)
                payload[d * CHUNK + CAPACITY] = both[0:4]
                payload[d * CHUNK + CAPACITY + 1] = both[4:8]
            return 0

        lax.fori_loop(0, tiles // 8, entries_of, 0)
        for copy in blanks:
            copy.wait()

    @pl.when(sec[0] != 0)
    def _():
        depth_copy = pltpu.make_async_copy(depth_in.at[0], depth, index_sem.at[0])
        depth_copy.start()
        copies = [
            pltpu.make_async_copy(field.at[0, :, pl.ds(lo, 8), :], edge.at[n], edge_sem.at[n])
            for n, (field, lo) in enumerate(
                ((temp, rows - 8), (merid, rows - 8), (temp, 0), (merid, 0))
            )
        ]
        for copy in copies:
            copy.start()

        def none(step, _):
            for j in range(UNROLL):
                slot_of[step * UNROLL + j] = 0
            return 0

        lax.fori_loop(0, blocks // UNROLL, none, 0)
        depth_copy.wait()
        for side, line in ((up, rows - 1), (down, 0)):
            side[2 * levels :, :] = jnp.broadcast_to(
                depth[line : line + 1, :].astype(f32), (8, depth.shape[1])
            )
        for n, copy in enumerate(copies):
            copy.wait()
            side = up if n < 2 else down
            side[pl.ds((n % 2) * levels, levels), :] = edge[n, :, 7 if n < 2 else 0, :]
        for side, brief in ((up, brief_up), (down, brief_down)):
            for m in range(3):
                brief[m : m + 1, :] = side[m * levels : m * levels + 1, :]


def through(k, depth, t, t_next, speed, speed_next):
    return jnp.where(
        k < depth,
        HEAT_DIFFUSION * (t_next - t) - (0.25 * (speed + speed_next)) * (t + t_next),
        0.0,
    )


def inner_faces(k, t, u, v, depth_e, depth_n):
    rows, cells = t.shape
    first = iota((rows, cells), 0) == 0
    east = through(k, depth_e, t, pltpu.roll(t, cells - 1, 1), u, pltpu.roll(u, cells - 1, 1))
    north = through(k, depth_n, t, pltpu.roll(t, rows - 1, 0), v, pltpu.roll(v, rows - 1, 0))
    return (east - pltpu.roll(east, 1, 1)) + (
        north - jnp.where(first, 0.0, pltpu.roll(north, 1, 0))
    )


def inner_depths(d):
    rows, cells = d.shape
    last = iota((rows, cells), 0) == rows - 1
    return (
        jnp.minimum(d, pltpu.roll(d, cells - 1, 1)),
        jnp.where(last, 0, jnp.minimum(d, pltpu.roll(d, rows - 1, 0))),
    )


def bring(copies):
    for copy in copies:
        copy.start()
    for copy in copies:
        copy.wait()


def surface_kernel(
    sec, temp, zonal, merid, depth, south, north,
    top,
    t_in, u_in, v_in, d_in, edge, made, sem, out_sem,
):
    @pl.when(sec[0] != 0)
    def _():
        pairs = [
            (temp.at[0, 0:2], t_in),
            (zonal.at[0, 0], u_in),
            (merid.at[0, 0], v_in),
            (depth.at[0], d_in),
            (north, edge.at[0]),
            (south, edge.at[1]),
        ]
        bring([pltpu.make_async_copy(*pair, sem.at[n]) for n, pair in enumerate(pairs)])
        d = d_in[...]
        rows, cells = d.shape
        t, v = t_in[0], v_in[...]
        t_n, v_n, d_n = (edge[0, m : m + 1, :] for m in range(3))
        t_s, v_s, d_s = (edge[1, m : m + 1, :] for m in range(3))
        end = slice(rows - 1, rows)
        northmost = through(
            0, jnp.minimum(d[end], d_n.astype(i32)), t[end], t_n, v[end], v_n
        )
        southmost = through(0, jnp.minimum(d[0:1], d_s.astype(i32)), t_s, t[0:1], v_s, v[0:1])
        at = iota((rows, cells), 0)
        outer = jnp.where(at == rows - 1, northmost, 0.0) - jnp.where(at == 0, southmost, 0.0)
        below = jnp.where(1 < d, VERTICAL_MIXING * (t_in[1] - t), 0.0)
        base = t + (inner_faces(0, t, u_in[...], v, *inner_depths(d)) + outer) + below
        wet = jnp.where(d > 0, FLUX_GAIN, 0.0)
        patches = cells // 128
        for p in range(patches):
            part = slice(p * 128, p * 128 + 128)
            made[0, pl.ds(p, rows, stride=patches), :] = t[:, part]
            made[1, pl.ds(p, rows, stride=patches), :] = base[:, part]
            made[2, pl.ds(p, rows, stride=patches), :] = wet[:, part]
        bring([pltpu.make_async_copy(made, top, out_sem)])


def ocean_kernel(
    levels, temp, zonal, merid, depth_in,
    out,
    depth, depth_e, depth_n, carry, sem,
):
    rows, cells = depth.shape
    bring([pltpu.make_async_copy(depth_in.at[0], depth, sem)])
    e, n = inner_depths(depth[...])
    depth_e[...] = e
    depth_n[...] = n
    carry[...] = jnp.zeros_like(carry)

    def step(index, temp_in, beneath, zonal_in, merid_in, fresh):
        i = index.index[0]
        above = carry[...]
        for j in range(LEVELS):
            k = i * LEVELS + j
            t = temp_in[0, j]
            under = beneath[0, 0] if j == LEVELS - 1 else temp_in[0, j + 1]
            below = jnp.where(k + 1 < depth[...], VERTICAL_MIXING * (under - t), 0.0)
            inner = inner_faces(k, t, zonal_in[0, j], merid_in[0, j], depth_e[...], depth_n[...])
            fresh[0, j] = t + inner + (below - above)
            above = below
        carry[...] = above

    slab = pl.BlockSpec((1, LEVELS, rows, cells), lambda i: (0, i, 0, 0))
    next_level = pl.BlockSpec(
        (1, 1, rows, cells), lambda i: (0, jnp.minimum((i + 1) * LEVELS, levels - 1), 0, 0)
    )
    pltpu.emit_pipeline(
        step,
        grid=(levels // LEVELS,),
        in_specs=[slab, next_level, slab, slab],
        out_specs=[slab],
        _explicit_indices=True,
    )(temp, temp, zonal, merid, out)


def settle_kernel(
    levels, sec, up_in, down_in, south_in, north_in, fresh_in, middle, blank,
    out,
    up, down, south, north, fresh, field, northmost, southmost, side_sem, in_sem, out_sem,
):
    rows, cells = field.shape[1:]
    patches = cells // 128

    @pl.when(sec[0] != 0)
    def _():
        pairs = (
            (up_in, up), (down_in, down), (south_in, south), (north_in, north), (fresh_in, fresh)
        )
        sides = [pltpu.make_async_copy(*pair, side_sem.at[n]) for n, pair in enumerate(pairs)]
        parts = [pl.ds(n * LEVELS, LEVELS) for n in range(levels // LEVELS)]
        ins = [
            pltpu.make_async_copy(middle.at[0, part], field.at[part], in_sem.at[n])
            for n, part in enumerate(parts)
        ]
        outs = [
            pltpu.make_async_copy(field.at[part], out.at[0, part], out_sem.at[n])
            for n, part in enumerate(parts)
        ]
        for copy in sides + ins:
            copy.start()
        for copy in sides:
            copy.wait()
        own_n = up[2 * levels : 2 * levels + 1, :].astype(i32)
        own_s = down[2 * levels : 2 * levels + 1, :].astype(i32)
        d_n = jnp.minimum(own_n, north[2 * levels : 2 * levels + 1, :].astype(i32))
        d_s = jnp.minimum(own_s, south[2 * levels : 2 * levels + 1, :].astype(i32))
        for at in range(0, levels, 8):
            k = iota((8, cells), 0) + at
            t, v = slice(at, at + 8), slice(levels + at, levels + at + 8)
            northmost[t, :] = through(k, d_n, up[t, :], north[t, :], up[v, :], north[v, :])
            southmost[t, :] = through(k, d_s, south[t, :], down[t, :], south[v, :], down[v, :])
        for n in range(len(parts)):
            ins[n].wait()
            for k in range(n * LEVELS, (n + 1) * LEVELS):
                field[k, rows - 1 : rows, :] += northmost[k : k + 1, :]
                field[k, 0:1, :] -= southmost[k : k + 1, :]
            if n == 0:
                for p in range(patches):
                    field[0, :, p * 128 : p * 128 + 128] = fresh[pl.ds(p, rows, stride=patches), :]
            outs[n].start()
        for copy in outs:
            copy.wait()


def in_three(x):
    high = x.astype(bf16)
    rest = x - high.astype(f32)
    middle = rest.astype(bf16)
    low = (rest - middle.astype(f32)).astype(bf16)
    return jnp.concatenate([high, middle, low], axis=1)


def joined(x, at=0):
    return x[:, at : at + 128] + (x[:, at + 128 : at + 256] + x[:, at + 256 : at + 384])


def heat_kernel(tiles, sec, payload, top, table, ret, fresh, hit, weighted):
    slots = tiles * CAPACITY

    @pl.when(sec[0] != 0)
    def _():
        ret[...] = jnp.zeros_like(ret)
        fresh[...] = jnp.zeros_like(fresh)

    @pl.when(sec[0] == 0)
    def _():
        surface_parts = in_three(top[0])
        table_parts = in_three(
            jnp.concatenate([table[...], jnp.zeros((128 - table.shape[0], 128), f32)], axis=0)
        )
        lane = iota((1, 8, 128), 2).astype(f32)
        group = min(64, tiles)

        def step(g, _):
            base = pl.multiple_of(g * group, group)
            upper = payload[pl.ds(base * CHUNK, group * CHUNK)].reshape(group, CHUNK, 4, 128)
            entry = upper[:, CAPACITY:].reshape(group, 8, 128)
            at = pl.multiple_of(base * CAPACITY, group * CAPACITY)
            size = group * CAPACITY
            block_hit = jnp.concatenate(
                [entry[:, None, :, 0:1] == lane[None], entry[:, None, :, 64:65] == lane[None]],
                axis=1,
            ).reshape(size, 128)
            row_hit = jnp.concatenate(
                [entry[:, None, :, 32:33] == lane[None], entry[:, None, :, 96:97] == lane[None]],
                axis=1,
            ).reshape(size, 128)
            live = jnp.concatenate(
                [
                    jnp.broadcast_to(entry[:, None, :, 0:1], (group, 1, 8, 128)),
                    jnp.broadcast_to(entry[:, None, :, 64:65], (group, 1, 8, 128)),
                ],
                axis=1,
            ).reshape(size, 128) >= 0
            block_one = jnp.where(block_hit, 1.0, 0.0).astype(bf16)
            row_one = jnp.where(row_hit, 1.0, 0.0).astype(bf16)
            hit[pl.ds(at, size), :] = block_one
            surface = joined(jnp.dot(block_one, surface_parts, preferred_element_type=f32))
            weights = joined(jnp.dot(row_one, table_parts, preferred_element_type=f32))

            def channel(c):
                return upper[:, :CAPACITY, c, :].reshape(size, 128)

            contrast = surface - channel(1)
            transfer = 0.8 + 0.4 * jnp.tanh(contrast)
            saturation = 0.6 * jnp.exp(0.3 * surface)
            heat = channel(3) - transfer * channel(0) * (
                contrast + 1.5 * (saturation - channel(2))
            )
            product = jnp.where(live, weights * heat, 0.0)
            weighted[pl.ds(at, size), 0:384] = in_three(product)
            weighted[pl.ds(at, size), 384:768] = in_three(weights)
            return 0

        lax.fori_loop(0, tiles // group, step, 0)
        sums = lax.dot_general(
            hit[...], weighted[...], (((0,), (0,)), ((), ())), preferred_element_type=f32
        )
        forcing = joined(sums) / jnp.maximum(joined(sums, 384), 1.0)
        new_top = top[1] + top[2] * forcing
        fresh[...] = new_top
        ret[...] = joined(jnp.dot(hit[...], in_three(new_top), preferred_element_type=f32))


def nothing_kernel(*refs):
    pass


def body(
    atm_state, routes, dst_block, weight_index, area_table, ocean_temp, vel_u, vel_v, depth_levels
):
    tiles = lax.axis_size("tile")
    block_count = atm_state.shape[1]
    levels, rows, cells = ocean_temp.shape[1:]
    patches = rows * cells // 128
    slots = tiles * CAPACITY
    sec = lax.axis_index("sec").astype(i32).reshape(1)
    grant = pltpu.CompilerParams(vmem_limit_bytes=24 << 20)
    ocean_grant = pltpu.CompilerParams(vmem_limit_bytes=56 << 20)
    whole_grant = pltpu.CompilerParams(vmem_limit_bytes=60 << 20)

    edge_rows = 2 * levels + 8
    payload, slot_of, up, down, brief_up, brief_down, blank = pl.pallas_call(
        functools.partial(pack_kernel, tiles),
        out_shape=(
            jax.ShapeDtypeStruct((tiles * CHUNK, 4, 128), f32),
            jax.ShapeDtypeStruct((block_count,), i32),
            jax.ShapeDtypeStruct((edge_rows, cells), f32),
            jax.ShapeDtypeStruct((edge_rows, cells), f32),
            jax.ShapeDtypeStruct((8, cells), f32),
            jax.ShapeDtypeStruct((8, cells), f32),
            jax.ShapeDtypeStruct(ocean_temp.shape, f32),
        ),
        in_specs=[SMEM] + [HBM] * 7,
        out_specs=(VMEM, SMEM, VMEM, VMEM, VMEM, VMEM, HBM),
        scratch_shapes=[
            pltpu.SMEM((block_count,), i32),
            pltpu.SMEM((block_count,), i32),
            pltpu.SMEM((block_count,), i32),
            pltpu.VMEM((block_count, 4, 128), f32),
            pltpu.SMEM((tiles,), i32),
            pltpu.VMEM((tiles * CHUNK, 128), i32),
            pltpu.VMEM((4, levels, 8, cells), f32),
            pltpu.VMEM((rows, cells), i32),
            pltpu.VMEM((LEVELS, rows, cells), f32),
            pltpu.SemaphoreType.DMA((3,)),
            pltpu.SemaphoreType.DMA((4,)),
            pltpu.SemaphoreType.DMA((4,)),
            pltpu.SemaphoreType.DMA((levels // LEVELS,)),
        ],
        compiler_params=whole_grant,
        name="pack",
    )(
        sec, routes.reshape(block_count), dst_block.reshape(block_count),
        weight_index.reshape(block_count), atm_state, depth_levels, ocean_temp, vel_v,
    )

    def unwritten(shapes):
        return pl.pallas_call(
            nothing_kernel,
            out_shape=shapes,
            out_specs=tuple(HBM for _ in shapes),
            compiler_params=ocean_grant,
            name="nothing",
        )()

    def from_sides(northmost, southmost):
        north_to = [(tiles + t, tiles + t + 1) for t in range(tiles - 1)]
        south_to = [(t + 1, t) for t in range(tiles, 2 * tiles - 1)]
        return (
            lax.ppermute(northmost, ("sec", "tile"), north_to),
            lax.ppermute(southmost, ("sec", "tile"), south_to),
        )

    top_shape = jax.ShapeDtypeStruct((3, patches, 128), f32)
    edge_shape = jax.ShapeDtypeStruct((edge_rows, cells), f32)
    field_shape = jax.ShapeDtypeStruct(ocean_temp.shape, f32)

    def split(atmosphere, ocean, *values):
        return lax.cond(sec[0] == 0, atmosphere, ocean, *values)

    def exchanged(value):
        return lax.all_to_all(value, "tile", split_axis=0, concat_axis=0, tiled=True)

    def surface(brief_up, brief_down):
        south, north = from_sides(brief_up, brief_down)
        return pl.pallas_call(
            surface_kernel,
            out_shape=top_shape,
            in_specs=[SMEM] + [HBM] * 4 + [ANY] * 2,
            out_specs=HBM,
            scratch_shapes=[
                pltpu.VMEM((2, rows, cells), f32),
                pltpu.VMEM((rows, cells), f32),
                pltpu.VMEM((rows, cells), f32),
                pltpu.VMEM((rows, cells), i32),
                pltpu.VMEM((2, 8, cells), f32),
                pltpu.VMEM((3, patches, 128), f32),
                pltpu.SemaphoreType.DMA((6,)),
                pltpu.SemaphoreType.DMA(()),
            ],
            compiler_params=ocean_grant,
            name="surface",
        )(sec, ocean_temp, vel_u, vel_v, depth_levels, south, north)

    def middle_of(temp, zonal, merid, depth):
        return pl.pallas_call(
            functools.partial(ocean_kernel, levels),
            in_specs=[HBM] * 4,
            out_specs=HBM,
            out_shape=field_shape,
            scratch_shapes=[
                pltpu.VMEM((rows, cells), i32),
                pltpu.VMEM((rows, cells), i32),
                pltpu.VMEM((rows, cells), i32),
                pltpu.VMEM((rows, cells), f32),
                pltpu.SemaphoreType.DMA(()),
            ],
            compiler_params=ocean_grant,
            name="ocean",
        )(temp, zonal, merid, depth)

    top = split(
        lambda up, down: unwritten((top_shape,))[0], surface, brief_up, brief_down
    )
    payload, up, down, top = lax.optimization_barrier((payload, up, down, top))
    top = lax.ppermute(top, "sec", [(1, 0)])

    def first_atmosphere(payload):
        payload, middle = lax.optimization_barrier((payload, unwritten((field_shape,))[0]))
        return exchanged(payload), middle

    moved, middle = split(
        first_atmosphere,
        lambda payload: (payload, middle_of(ocean_temp, vel_u, vel_v, depth_levels)),
        payload,
    )

    ret, fresh = pl.pallas_call(
        functools.partial(heat_kernel, tiles),
        out_shape=(
            jax.ShapeDtypeStruct((slots, 128), f32),
            jax.ShapeDtypeStruct((patches, 128), f32),
        ),
        in_specs=[SMEM, VMEM, VMEM, VMEM],
        out_specs=(VMEM, VMEM),
        scratch_shapes=[pltpu.VMEM((slots, 128), bf16), pltpu.VMEM((slots, 768), bf16)],
        compiler_params=grant,
        name="heat",
    )(sec, moved, top, area_table)
    fresh = lax.ppermute(fresh, "sec", [(0, 1)])

    def second_atmosphere(ret, up, down):
        ret, south, north = lax.optimization_barrier((ret, *unwritten((edge_shape, edge_shape))))
        return exchanged(ret), south, north

    back, south, north = split(
        second_atmosphere, lambda ret, up, down: (ret, *from_sides(up, down)), ret, up, down
    )
    index = slot_of - (CHUNK - CAPACITY) * (slot_of // CHUNK)
    whole_rows = lax.GatherDimensionNumbers(
        offset_dims=(1,), collapsed_slice_dims=(0,), start_index_map=(0,)
    )
    skin = lax.gather(
        back, index[:, None], whole_rows, (1, 128),
        mode=lax.GatherScatterMode.PROMISE_IN_BOUNDS,
    )
    following = pl.pallas_call(
        functools.partial(settle_kernel, levels),
        out_shape=field_shape,
        in_specs=[SMEM] + [ANY] * 5 + [HBM] * 2,
        out_specs=HBM,
        scratch_shapes=[pltpu.VMEM((edge_rows, cells), f32)] * 4
        + [
            pltpu.VMEM((patches, 128), f32),
            pltpu.VMEM((levels, rows, cells), f32),
            pltpu.VMEM((levels, cells), f32),
            pltpu.VMEM((levels, cells), f32),
            pltpu.SemaphoreType.DMA((5,)),
            pltpu.SemaphoreType.DMA((levels // LEVELS,)),
            pltpu.SemaphoreType.DMA((levels // LEVELS,)),
        ],
        input_output_aliases={7: 0},
        compiler_params=grant,
        name="settle",
    )(sec, up, down, south, north, fresh, middle, blank)
    return following, skin[None]


def solution(mesh):
    return jax.shard_map(
        body,
        mesh=mesh,
        in_specs=(
            P("sec", "tile", None, None),
            P("sec", "tile", None),
            P("sec", "tile"),
            P("sec", "tile"),
            P(),
            P("sec", None, "tile", None),
            P("sec", None, "tile", None),
            P("sec", None, "tile", None),
            P("sec", "tile", None),
        ),
        out_specs=(P("sec", None, "tile", None), P("sec", "tile", None)),
        check_vma=False,
    )
```

```python
import functools

import jax
import jax.numpy as jnp
from jax import lax
from jax.experimental import pallas as pl
from jax.experimental.pallas import tpu as pltpu
from jax.sharding import PartitionSpec as P

HEAT_DIFFUSION = 0.12
VERTICAL_MIXING = 0.2
FLUX_GAIN = 0.5
CAPACITY = 16
CHUNK = CAPACITY + 1
UNROLL = 16
LEVELS = 16

f32, bf16, i32 = jnp.float32, jnp.bfloat16, jnp.int32
VMEM = pl.BlockSpec(memory_space=pltpu.VMEM)
SMEM = pl.BlockSpec(memory_space=pltpu.SMEM)
ANY = pl.BlockSpec(memory_space=pl.ANY)
HBM = pl.BlockSpec(memory_space=pltpu.HBM)


def iota(shape, axis):
    return lax.broadcasted_iota(i32, shape, axis)


def pack_kernel(
    tiles, sec, dest_in, block_in, row_in, state_in, depth_in, temp, merid,
    payload, slot_of, up, down, brief_up, brief_down, blank,
    dest, block, row, state, count, entry, edge, depth,
    nothing, index_sem, state_sem, edge_sem, blank_sem,
):
    levels = temp.shape[1]
    rows = temp.shape[2]
    blocks = dest.shape[0]
    pieces = state_sem.shape[0]
    piece = blocks // pieces

    @pl.when(sec[0] == 0)
    def _():
        indices = [
            pltpu.make_async_copy(source, target, index_sem.at[n])
            for n, (source, target) in enumerate(
                ((dest_in, dest), (block_in, block), (row_in, row))
            )
        ]
        states = [
            pltpu.make_async_copy(
                state_in.at[0, pl.ds(n * piece, piece)],
                state.at[pl.ds(n * piece, piece)],
                state_sem.at[n],
            )
            for n in range(pieces)
        ]
        for copy in indices + states:
            copy.start()
        nothing[...] = jnp.zeros_like(nothing)
        blanks = [
            pltpu.make_async_copy(
                nothing, blank.at[0, pl.ds(n * LEVELS, LEVELS)], blank_sem.at[n]
            )
            for n in range(levels // LEVELS)
        ]
        for copy in blanks:
            copy.start()

        for i in range(tiles):
            count[i] = i * CHUNK
        entry[...] = jnp.full(entry.shape, -1, i32)
        is_block = (iota((1, 128), 1) & 16) == 0
        for copy in indices:
            copy.wait()

        def place(step, _):
            for j in range(UNROLL):
                i = step * UNROLL + j
                d = dest[i]
                place_of = count[d]
                count[d] = place_of + 1
                slot_of[i] = place_of
                payload[place_of] = state[i]
                entry[pl.ds(place_of, 1), :] = jnp.where(is_block, block[i], row[i])
            return 0

        for n in range(pieces):
            states[n].wait()
            lax.fori_loop(n * piece // UNROLL, (n + 1) * piece // UNROLL, place, 0)
        quarter = iota((4, 128), 1) // 32

        def entries_of(g, _):
            for j in range(8):
                d = g * 8 + j
                both = entry[pl.ds(d * CHUNK, 4), :]
                for q in range(1, 4):
                    both = jnp.where(quarter == q, entry[pl.ds(d * CHUNK + 4 * q, 4), :], both)
                payload[d * CHUNK + CAPACITY] = both.astype(f32)
            return 0

        lax.fori_loop(0, tiles // 8, entries_of, 0)
        for copy in blanks:
            copy.wait()

    @pl.when(sec[0] != 0)
    def _():
        depth_copy = pltpu.make_async_copy(depth_in.at[0], depth, index_sem.at[0])
        depth_copy.start()
        copies = [
            pltpu.make_async_copy(field.at[0, :, pl.ds(lo, 8), :], edge.at[n], edge_sem.at[n])
            for n, (field, lo) in enumerate(
                ((temp, rows - 8), (merid, rows - 8), (temp, 0), (merid, 0))
            )
        ]
        for copy in copies:
            copy.start()

        def none(step, _):
            for j in range(UNROLL):
                slot_of[step * UNROLL + j] = 0
            return 0

        lax.fori_loop(0, blocks // UNROLL, none, 0)
        depth_copy.wait()
        for side, line in ((up, rows - 1), (down, 0)):
            side[2 * levels :, :] = jnp.broadcast_to(
                depth[line : line + 1, :].astype(f32), (8, depth.shape[1])
            )
        for n, copy in enumerate(copies):
            copy.wait()
            side = up if n < 2 else down
            side[pl.ds((n % 2) * levels, levels), :] = edge[n, :, 7 if n < 2 else 0, :]
        for side, brief in ((up, brief_up), (down, brief_down)):
            for m in range(3):
                brief[m : m + 1, :] = side[m * levels : m * levels + 1, :]


def through(k, depth, t, t_next, speed, speed_next):
    return jnp.where(
        k < depth,
        HEAT_DIFFUSION * (t_next - t) - (0.25 * (speed + speed_next)) * (t + t_next),
        0.0,
    )


def inner_faces(k, t, u, v, depth_e, depth_n):
    rows, cells = t.shape
    first = iota((rows, cells), 0) == 0
    east = through(k, depth_e, t, pltpu.roll(t, cells - 1, 1), u, pltpu.roll(u, cells - 1, 1))
    north = through(k, depth_n, t, pltpu.roll(t, rows - 1, 0), v, pltpu.roll(v, rows - 1, 0))
    return (east - pltpu.roll(east, 1, 1)) + (
        north - jnp.where(first, 0.0, pltpu.roll(north, 1, 0))
    )


def inner_depths(d):
    rows, cells = d.shape
    last = iota((rows, cells), 0) == rows - 1
    return (
        jnp.minimum(d, pltpu.roll(d, cells - 1, 1)),
        jnp.where(last, 0, jnp.minimum(d, pltpu.roll(d, rows - 1, 0))),
    )


def bring(copies):
    for copy in copies:
        copy.start()
    for copy in copies:
        copy.wait()


def surface_kernel(
    sec, temp, zonal, merid, depth, south, north,
    top,
    t_in, u_in, v_in, d_in, edge, made, sem, out_sem,
):
    @pl.when(sec[0] != 0)
    def _():
        pairs = [
            (temp.at[0, 0:2], t_in),
            (zonal.at[0, 0], u_in),
            (merid.at[0, 0], v_in),
            (depth.at[0], d_in),
            (north, edge.at[0]),
            (south, edge.at[1]),
        ]
        bring([pltpu.make_async_copy(*pair, sem.at[n]) for n, pair in enumerate(pairs)])
        d = d_in[...]
        rows, cells = d.shape
        t, v = t_in[0], v_in[...]
        t_n, v_n, d_n = (edge[0, m : m + 1, :] for m in range(3))
        t_s, v_s, d_s = (edge[1, m : m + 1, :] for m in range(3))
        end = slice(rows - 1, rows)
        northmost = through(
            0, jnp.minimum(d[end], d_n.astype(i32)), t[end], t_n, v[end], v_n
        )
        southmost = through(0, jnp.minimum(d[0:1], d_s.astype(i32)), t_s, t[0:1], v_s, v[0:1])
        at = iota((rows, cells), 0)
        outer = jnp.where(at == rows - 1, northmost, 0.0) - jnp.where(at == 0, southmost, 0.0)
        below = jnp.where(1 < d, VERTICAL_MIXING * (t_in[1] - t), 0.0)
        base = t + (inner_faces(0, t, u_in[...], v, *inner_depths(d)) + outer) + below
        wet = jnp.where(d > 0, FLUX_GAIN, 0.0)
        patches = cells // 128
        for p in range(patches):
            part = slice(p * 128, p * 128 + 128)
            made[0, pl.ds(p, rows, stride=patches), :] = t[:, part]
            made[1, pl.ds(p, rows, stride=patches), :] = base[:, part]
            made[2, pl.ds(p, rows, stride=patches), :] = wet[:, part]
        bring([pltpu.make_async_copy(made, top, out_sem)])


def ocean_kernel(
    levels, temp, zonal, merid, depth_in,
    out,
    depth, depth_e, depth_n, carry, sem,
):
    rows, cells = depth.shape
    bring([pltpu.make_async_copy(depth_in.at[0], depth, sem)])
    e, n = inner_depths(depth[...])
    depth_e[...] = e
    depth_n[...] = n
    carry[...] = jnp.zeros_like(carry)

    def step(index, temp_in, beneath, zonal_in, merid_in, fresh):
        i = index.index[0]
        above = carry[...]
        for j in range(LEVELS):
            k = i * LEVELS + j
            t = temp_in[0, j]
            under = beneath[0, 0] if j == LEVELS - 1 else temp_in[0, j + 1]
            below = jnp.where(k + 1 < depth[...], VERTICAL_MIXING * (under - t), 0.0)
            inner = inner_faces(k, t, zonal_in[0, j], merid_in[0, j], depth_e[...], depth_n[...])
            fresh[0, j] = t + inner + (below - above)
            above = below
        carry[...] = above

    slab = pl.BlockSpec((1, LEVELS, rows, cells), lambda i: (0, i, 0, 0))
    next_level = pl.BlockSpec(
        (1, 1, rows, cells), lambda i: (0, jnp.minimum((i + 1) * LEVELS, levels - 1), 0, 0)
    )
    pltpu.emit_pipeline(
        step,
        grid=(levels // LEVELS,),
        in_specs=[slab, next_level, slab, slab],
        out_specs=[slab],
        _explicit_indices=True,
    )(temp, temp, zonal, merid, out)


def settle_kernel(
    levels, sec, up_in, down_in, south_in, north_in, fresh_in, middle, blank,
    out,
    up, down, south, north, fresh, field, northmost, southmost, side_sem, in_sem, out_sem,
):
    rows, cells = field.shape[1:]
    patches = cells // 128

    @pl.when(sec[0] != 0)
    def _():
        pairs = (
            (up_in, up), (down_in, down), (south_in, south), (north_in, north), (fresh_in, fresh)
        )
        sides = [pltpu.make_async_copy(*pair, side_sem.at[n]) for n, pair in enumerate(pairs)]
        parts = [pl.ds(n * LEVELS, LEVELS) for n in range(levels // LEVELS)]
        ins = [
            pltpu.make_async_copy(middle.at[0, part], field.at[part], in_sem.at[n])
            for n, part in enumerate(parts)
        ]
        outs = [
            pltpu.make_async_copy(field.at[part], out.at[0, part], out_sem.at[n])
            for n, part in enumerate(parts)
        ]
        for copy in sides + ins:
            copy.start()
        for copy in sides:
            copy.wait()
        own_n = up[2 * levels : 2 * levels + 1, :].astype(i32)
        own_s = down[2 * levels : 2 * levels + 1, :].astype(i32)
        d_n = jnp.minimum(own_n, north[2 * levels : 2 * levels + 1, :].astype(i32))
        d_s = jnp.minimum(own_s, south[2 * levels : 2 * levels + 1, :].astype(i32))
        for at in range(0, levels, 8):
            k = iota((8, cells), 0) + at
            t, v = slice(at, at + 8), slice(levels + at, levels + at + 8)
            northmost[t, :] = through(k, d_n, up[t, :], north[t, :], up[v, :], north[v, :])
            southmost[t, :] = through(k, d_s, south[t, :], down[t, :], south[v, :], down[v, :])
        for n in range(len(parts)):
            ins[n].wait()
            for k in range(n * LEVELS, (n + 1) * LEVELS):
                field[k, rows - 1 : rows, :] += northmost[k : k + 1, :]
                field[k, 0:1, :] -= southmost[k : k + 1, :]
            if n == 0:
                for p in range(patches):
                    field[0, :, p * 128 : p * 128 + 128] = fresh[pl.ds(p, rows, stride=patches), :]
            outs[n].start()
        for copy in outs:
            copy.wait()


def in_three(x):
    high = x.astype(bf16)
    rest = x - high.astype(f32)
    middle = rest.astype(bf16)
    low = (rest - middle.astype(f32)).astype(bf16)
    return jnp.concatenate([high, middle, low], axis=1)


def joined(x, at=0):
    return x[:, at : at + 128] + (x[:, at + 128 : at + 256] + x[:, at + 256 : at + 384])


def heat_kernel(tiles, sec, payload, top, table, ret, fresh, hit, weighted):
    slots = tiles * CAPACITY

    @pl.when(sec[0] != 0)
    def _():
        ret[...] = jnp.zeros_like(ret)
        fresh[...] = jnp.zeros_like(fresh)

    @pl.when(sec[0] == 0)
    def _():
        surface_parts = in_three(top[0])
        table_parts = in_three(
            jnp.concatenate([table[...], jnp.zeros((128 - table.shape[0], 128), f32)], axis=0)
        )
        lane = iota((1, 4, 128), 2).astype(f32)
        group = min(64, tiles)

        def step(g, _):
            base = pl.multiple_of(g * group, group)
            upper = payload[pl.ds(base * CHUNK, group * CHUNK)].reshape(group, CHUNK, 4, 128)
            entry = upper[:, CAPACITY]
            at = pl.multiple_of(base * CAPACITY, group * CAPACITY)
            size = group * CAPACITY

            def named(offset):
                return jnp.concatenate(
                    [
                        jnp.where(
                            entry[:, None, :, 32 * q + offset : 32 * q + offset + 1] == lane[None],
                            1.0, 0.0,
                        )
                        for q in range(4)
                    ],
                    axis=1,
                ).reshape(size, 128)

            block_hit = named(0)
            block_one = block_hit.astype(bf16)
            row_one = named(16).astype(bf16)
            live = jnp.sum(block_hit, axis=1, keepdims=True) > 0
            hit[pl.ds(at, size), :] = block_one
            surface = joined(jnp.dot(block_one, surface_parts, preferred_element_type=f32))
            weights = joined(jnp.dot(row_one, table_parts, preferred_element_type=f32))

            def channel(c):
                return upper[:, :CAPACITY, c, :].reshape(size, 128)

            contrast = surface - channel(1)
            transfer = 0.8 + 0.4 * jnp.tanh(contrast)
            saturation = 0.6 * jnp.exp(0.3 * surface)
            heat = channel(3) - transfer * channel(0) * (
                contrast + 1.5 * (saturation - channel(2))
            )
            product = jnp.where(live, weights * heat, 0.0)
            weighted[pl.ds(at, size), 0:384] = in_three(product)
            weighted[pl.ds(at, size), 384:768] = in_three(weights)
            return 0

        lax.fori_loop(0, tiles // group, step, 0)
        sums = lax.dot_general(
            hit[...], weighted[...], (((0,), (0,)), ((), ())), preferred_element_type=f32
        )
        forcing = joined(sums) / jnp.maximum(joined(sums, 384), 1.0)
        new_top = top[1] + top[2] * forcing
        fresh[...] = new_top
        ret[...] = joined(jnp.dot(hit[...], in_three(new_top), preferred_element_type=f32))


def nothing_kernel(*refs):
    pass


def body(
    atm_state, routes, dst_block, weight_index, area_table, ocean_temp, vel_u, vel_v, depth_levels
):
    tiles = lax.axis_size("tile")
    block_count = atm_state.shape[1]
    levels, rows, cells = ocean_temp.shape[1:]
    patches = rows * cells // 128
    slots = tiles * CAPACITY
    sec = lax.axis_index("sec").astype(i32).reshape(1)
    grant = pltpu.CompilerParams(vmem_limit_bytes=24 << 20)
    ocean_grant = pltpu.CompilerParams(vmem_limit_bytes=56 << 20)
    whole_grant = pltpu.CompilerParams(vmem_limit_bytes=60 << 20)

    edge_rows = 2 * levels + 8
    payload, slot_of, up, down, brief_up, brief_down, blank = pl.pallas_call(
        functools.partial(pack_kernel, tiles),
        out_shape=(
            jax.ShapeDtypeStruct((tiles * CHUNK, 4, 128), f32),
            jax.ShapeDtypeStruct((block_count,), i32),
            jax.ShapeDtypeStruct((edge_rows, cells), f32),
            jax.ShapeDtypeStruct((edge_rows, cells), f32),
            jax.ShapeDtypeStruct((8, cells), f32),
            jax.ShapeDtypeStruct((8, cells), f32),
            jax.ShapeDtypeStruct(ocean_temp.shape, f32),
        ),
        in_specs=[SMEM] + [HBM] * 7,
        out_specs=(VMEM, SMEM, VMEM, VMEM, VMEM, VMEM, HBM),
        scratch_shapes=[
            pltpu.SMEM((block_count,), i32),
            pltpu.SMEM((block_count,), i32),
            pltpu.SMEM((block_count,), i32),
            pltpu.VMEM((block_count, 4, 128), f32),
            pltpu.SMEM((tiles,), i32),
            pltpu.VMEM((tiles * CHUNK, 128), i32),
            pltpu.VMEM((4, levels, 8, cells), f32),
            pltpu.VMEM((rows, cells), i32),
            pltpu.VMEM((LEVELS, rows, cells), f32),
            pltpu.SemaphoreType.DMA((3,)),
            pltpu.SemaphoreType.DMA((4,)),
            pltpu.SemaphoreType.DMA((4,)),
            pltpu.SemaphoreType.DMA((levels // LEVELS,)),
        ],
        compiler_params=whole_grant,
        name="pack",
    )(
        sec, routes.reshape(block_count), dst_block.reshape(block_count),
        weight_index.reshape(block_count), atm_state, depth_levels, ocean_temp, vel_v,
    )

    def unwritten(shapes):
        return pl.pallas_call(
            nothing_kernel,
            out_shape=shapes,
            out_specs=tuple(HBM for _ in shapes),
            compiler_params=ocean_grant,
            name="nothing",
        )()

    def from_sides(northmost, southmost):
        north_to = [(tiles + t, tiles + t + 1) for t in range(tiles - 1)]
        south_to = [(t + 1, t) for t in range(tiles, 2 * tiles - 1)]
        return (
            lax.ppermute(northmost, ("sec", "tile"), north_to),
            lax.ppermute(southmost, ("sec", "tile"), south_to),
        )

    top_shape = jax.ShapeDtypeStruct((3, patches, 128), f32)
    edge_shape = jax.ShapeDtypeStruct((edge_rows, cells), f32)
    field_shape = jax.ShapeDtypeStruct(ocean_temp.shape, f32)

    def split(atmosphere, ocean, *values):
        return lax.cond(sec[0] == 0, atmosphere, ocean, *values)

    def exchanged(value):
        return lax.all_to_all(value, "tile", split_axis=0, concat_axis=0, tiled=True)

    def surface(brief_up, brief_down):
        south, north = from_sides(brief_up, brief_down)
        return pl.pallas_call(
            surface_kernel,
            out_shape=top_shape,
            in_specs=[SMEM] + [HBM] * 4 + [ANY] * 2,
            out_specs=HBM,
            scratch_shapes=[
                pltpu.VMEM((2, rows, cells), f32),
                pltpu.VMEM((rows, cells), f32),
                pltpu.VMEM((rows, cells), f32),
                pltpu.VMEM((rows, cells), i32),
                pltpu.VMEM((2, 8, cells), f32),
                pltpu.VMEM((3, patches, 128), f32),
                pltpu.SemaphoreType.DMA((6,)),
                pltpu.SemaphoreType.DMA(()),
            ],
            compiler_params=ocean_grant,
            name="surface",
        )(sec, ocean_temp, vel_u, vel_v, depth_levels, south, north)

    def middle_of(temp, zonal, merid, depth):
        return pl.pallas_call(
            functools.partial(ocean_kernel, levels),
            in_specs=[HBM] * 4,
            out_specs=HBM,
            out_shape=field_shape,
            scratch_shapes=[
                pltpu.VMEM((rows, cells), i32),
                pltpu.VMEM((rows, cells), i32),
                pltpu.VMEM((rows, cells), i32),
                pltpu.VMEM((rows, cells), f32),
                pltpu.SemaphoreType.DMA(()),
            ],
            compiler_params=ocean_grant,
            name="ocean",
        )(temp, zonal, merid, depth)

    top = split(
        lambda up, down: unwritten((top_shape,))[0], surface, brief_up, brief_down
    )
    payload, up, down, top = lax.optimization_barrier((payload, up, down, top))
    top = lax.ppermute(top, "sec", [(1, 0)])

    def first_atmosphere(payload):
        payload, middle = lax.optimization_barrier((payload, unwritten((field_shape,))[0]))
        return exchanged(payload), middle

    moved, middle = split(
        first_atmosphere,
        lambda payload: (payload, middle_of(ocean_temp, vel_u, vel_v, depth_levels)),
        payload,
    )

    ret, fresh = pl.pallas_call(
        functools.partial(heat_kernel, tiles),
        out_shape=(
            jax.ShapeDtypeStruct((slots, 128), f32),
            jax.ShapeDtypeStruct((patches, 128), f32),
        ),
        in_specs=[SMEM, VMEM, VMEM, VMEM],
        out_specs=(VMEM, VMEM),
        scratch_shapes=[pltpu.VMEM((slots, 128), bf16), pltpu.VMEM((slots, 768), bf16)],
        compiler_params=grant,
        name="heat",
    )(sec, moved, top, area_table)
    fresh = lax.ppermute(fresh, "sec", [(0, 1)])

    def second_atmosphere(ret, up, down):
        ret, south, north = lax.optimization_barrier((ret, *unwritten((edge_shape, edge_shape))))
        return exchanged(ret), south, north

    back, south, north = split(
        second_atmosphere, lambda ret, up, down: (ret, *from_sides(up, down)), ret, up, down
    )
    index = slot_of - (CHUNK - CAPACITY) * (slot_of // CHUNK)
    whole_rows = lax.GatherDimensionNumbers(
        offset_dims=(1,), collapsed_slice_dims=(0,), start_index_map=(0,)
    )
    skin = split(
        lambda back, index: lax.gather(
            back, index[:, None], whole_rows, (1, 128),
            mode=lax.GatherScatterMode.PROMISE_IN_BOUNDS,
        ),
        lambda back, index: back[:block_count],
        back, index,
    )
    following = pl.pallas_call(
        functools.partial(settle_kernel, levels),
        out_shape=field_shape,
        in_specs=[SMEM] + [ANY] * 5 + [HBM] * 2,
        out_specs=HBM,
        scratch_shapes=[pltpu.VMEM((edge_rows, cells), f32)] * 4
        + [
            pltpu.VMEM((patches, 128), f32),
            pltpu.VMEM((levels, rows, cells), f32),
            pltpu.VMEM((levels, cells), f32),
            pltpu.VMEM((levels, cells), f32),
            pltpu.SemaphoreType.DMA((5,)),
            pltpu.SemaphoreType.DMA((levels // LEVELS,)),
            pltpu.SemaphoreType.DMA((levels // LEVELS,)),
        ],
        input_output_aliases={7: 0},
        compiler_params=grant,
        name="settle",
    )(sec, up, down, south, north, fresh, middle, blank)
    return following, skin[None]


def solution(mesh):
    return jax.shard_map(
        body,
        mesh=mesh,
        in_specs=(
            P("sec", "tile", None, None),
            P("sec", "tile", None),
            P("sec", "tile"),
            P("sec", "tile"),
            P(),
            P("sec", None, "tile", None),
            P("sec", None, "tile", None),
            P("sec", None, "tile", None),
            P("sec", "tile", None),
        ),
        out_specs=(P("sec", None, "tile", None), P("sec", "tile", None)),
        check_vma=False,
    )
```

```python
import functools

import jax
import jax.numpy as jnp
from jax import lax
from jax.experimental import pallas as pl
from jax.experimental.pallas import tpu as pltpu
from jax.sharding import PartitionSpec as P

HEAT_DIFFUSION = 0.12
VERTICAL_MIXING = 0.2
FLUX_GAIN = 0.5
CAPACITY = 16
CHUNK = CAPACITY + 1
UNROLL = 16
LEVELS = 16

f32, bf16, i32 = jnp.float32, jnp.bfloat16, jnp.int32
VMEM = pl.BlockSpec(memory_space=pltpu.VMEM)
SMEM = pl.BlockSpec(memory_space=pltpu.SMEM)
ANY = pl.BlockSpec(memory_space=pl.ANY)
HBM = pl.BlockSpec(memory_space=pltpu.HBM)


def iota(shape, axis):
    return lax.broadcasted_iota(i32, shape, axis)


def pack_kernel(
    tiles, sec, dest_in, block_in, row_in, state_in, depth_in, temp, merid,
    payload, slot_of, up, down, brief_up, brief_down, blank,
    dest, block, row, state, count, entry, edge, depth,
    nothing, index_sem, state_sem, edge_sem, blank_sem,
):
    levels = temp.shape[1]
    rows = temp.shape[2]
    blocks = dest.shape[0]
    pieces = state_sem.shape[0]
    piece = blocks // pieces

    @pl.when(sec[0] == 0)
    def _():
        indices = [
            pltpu.make_async_copy(source, target, index_sem.at[n])
            for n, (source, target) in enumerate(
                ((dest_in, dest), (block_in, block), (row_in, row))
            )
        ]
        states = [
            pltpu.make_async_copy(
                state_in.at[0, pl.ds(n * piece, piece)],
                state.at[pl.ds(n * piece, piece)],
                state_sem.at[n],
            )
            for n in range(pieces)
        ]
        for copy in indices + states:
            copy.start()
        nothing[...] = jnp.zeros_like(nothing)
        blanks = [
            pltpu.make_async_copy(
                nothing, blank.at[0, pl.ds(n * LEVELS, LEVELS)], blank_sem.at[n]
            )
            for n in range(levels // LEVELS)
        ]
        for copy in blanks:
            copy.start()

        for i in range(tiles):
            count[i] = i * CHUNK
        entry[...] = jnp.full(entry.shape, -1, i32)
        is_block = (iota((1, 128), 1) & 16) == 0
        for copy in indices:
            copy.wait()

        def place(step, _):
            for j in range(UNROLL):
                i = step * UNROLL + j
                d = dest[i]
                place_of = count[d]
                count[d] = place_of + 1
                slot_of[i] = place_of
                payload[place_of] = state[i]
                entry[pl.ds(place_of, 1), :] = jnp.where(is_block, block[i], row[i])
            return 0

        for n in range(pieces):
            states[n].wait()
            lax.fori_loop(n * piece // UNROLL, (n + 1) * piece // UNROLL, place, 0)
        quarter = iota((4, 128), 1) // 32

        def entries_of(g, _):
            for j in range(8):
                d = g * 8 + j
                both = entry[pl.ds(d * CHUNK, 4), :]
                for q in range(1, 4):
                    both = jnp.where(quarter == q, entry[pl.ds(d * CHUNK + 4 * q, 4), :], both)
                payload[d * CHUNK + CAPACITY] = both.astype(f32)
            return 0

        lax.fori_loop(0, tiles // 8, entries_of, 0)
        for copy in blanks:
            copy.wait()

    @pl.when(sec[0] != 0)
    def _():
        depth_copy = pltpu.make_async_copy(depth_in.at[0], depth, index_sem.at[0])
        depth_copy.start()
        copies = [
            pltpu.make_async_copy(field.at[0, :, pl.ds(lo, 8), :], edge.at[n], edge_sem.at[n])
            for n, (field, lo) in enumerate(
                ((temp, rows - 8), (merid, rows - 8), (temp, 0), (merid, 0))
            )
        ]
        for copy in copies:
            copy.start()

        def none(step, _):
            for j in range(UNROLL):
                slot_of[step * UNROLL + j] = 0
            return 0

        lax.fori_loop(0, blocks // UNROLL, none, 0)
        depth_copy.wait()
        for side, line in ((up, rows - 1), (down, 0)):
            side[2 * levels :, :] = jnp.broadcast_to(
                depth[line : line + 1, :].astype(f32), (8, depth.shape[1])
            )
        for n, copy in enumerate(copies):
            copy.wait()
            side = up if n < 2 else down
            side[pl.ds((n % 2) * levels, levels), :] = edge[n, :, 7 if n < 2 else 0, :]
        for side, brief in ((up, brief_up), (down, brief_down)):
            for m in range(3):
                brief[m : m + 1, :] = side[m * levels : m * levels + 1, :]


def through(k, depth, t, t_next, speed, speed_next):
    return jnp.where(
        k < depth,
        HEAT_DIFFUSION * (t_next - t) - (0.25 * (speed + speed_next)) * (t + t_next),
        0.0,
    )


def inner_faces(k, t, u, v, depth_e, depth_n):
    rows, cells = t.shape
    first = iota((rows, cells), 0) == 0
    east = through(k, depth_e, t, pltpu.roll(t, cells - 1, 1), u, pltpu.roll(u, cells - 1, 1))
    north = through(k, depth_n, t, pltpu.roll(t, rows - 1, 0), v, pltpu.roll(v, rows - 1, 0))
    return (east - pltpu.roll(east, 1, 1)) + (
        north - jnp.where(first, 0.0, pltpu.roll(north, 1, 0))
    )


def inner_depths(d):
    rows, cells = d.shape
    last = iota((rows, cells), 0) == rows - 1
    return (
        jnp.minimum(d, pltpu.roll(d, cells - 1, 1)),
        jnp.where(last, 0, jnp.minimum(d, pltpu.roll(d, rows - 1, 0))),
    )


def bring(copies):
    for copy in copies:
        copy.start()
    for copy in copies:
        copy.wait()


def surface_kernel(
    sec, temp, zonal, merid, depth, south, north,
    top,
    t_in, u_in, v_in, d_in, edge, made, sem, out_sem,
):
    @pl.when(sec[0] != 0)
    def _():
        pairs = [
            (temp.at[0, 0:2], t_in),
            (zonal.at[0, 0], u_in),
            (merid.at[0, 0], v_in),
            (depth.at[0], d_in),
            (north, edge.at[0]),
            (south, edge.at[1]),
        ]
        bring([pltpu.make_async_copy(*pair, sem.at[n]) for n, pair in enumerate(pairs)])
        d = d_in[...]
        rows, cells = d.shape
        t, v = t_in[0], v_in[...]
        t_n, v_n, d_n = (edge[0, m : m + 1, :] for m in range(3))
        t_s, v_s, d_s = (edge[1, m : m + 1, :] for m in range(3))
        end = slice(rows - 1, rows)
        northmost = through(
            0, jnp.minimum(d[end], d_n.astype(i32)), t[end], t_n, v[end], v_n
        )
        southmost = through(0, jnp.minimum(d[0:1], d_s.astype(i32)), t_s, t[0:1], v_s, v[0:1])
        at = iota((rows, cells), 0)
        outer = jnp.where(at == rows - 1, northmost, 0.0) - jnp.where(at == 0, southmost, 0.0)
        below = jnp.where(1 < d, VERTICAL_MIXING * (t_in[1] - t), 0.0)
        base = t + (inner_faces(0, t, u_in[...], v, *inner_depths(d)) + outer) + below
        wet = jnp.where(d > 0, FLUX_GAIN, 0.0)
        patches = cells // 128
        for p in range(patches):
            part = slice(p * 128, p * 128 + 128)
            made[0, pl.ds(p, rows, stride=patches), :] = t[:, part]
            made[1, pl.ds(p, rows, stride=patches), :] = base[:, part]
            made[2, pl.ds(p, rows, stride=patches), :] = wet[:, part]
        bring([pltpu.make_async_copy(made, top, out_sem)])


def ocean_kernel(
    levels, temp, zonal, merid, depth_in,
    out,
    depth, depth_e, depth_n, carry, sem,
):
    rows, cells = depth.shape
    bring([pltpu.make_async_copy(depth_in.at[0], depth, sem)])
    e, n = inner_depths(depth[...])
    depth_e[...] = e
    depth_n[...] = n
    carry[...] = jnp.zeros_like(carry)

    def step(index, temp_in, beneath, zonal_in, merid_in, fresh):
        i = index.index[0]
        above = carry[...]
        for j in range(LEVELS):
            k = i * LEVELS + j
            t = temp_in[0, j]
            under = beneath[0, 0] if j == LEVELS - 1 else temp_in[0, j + 1]
            below = jnp.where(k + 1 < depth[...], VERTICAL_MIXING * (under - t), 0.0)
            inner = inner_faces(k, t, zonal_in[0, j], merid_in[0, j], depth_e[...], depth_n[...])
            fresh[0, j] = t + inner + (below - above)
            above = below
        carry[...] = above

    slab = pl.BlockSpec((1, LEVELS, rows, cells), lambda i: (0, i, 0, 0))
    next_level = pl.BlockSpec(
        (1, 1, rows, cells), lambda i: (0, jnp.minimum((i + 1) * LEVELS, levels - 1), 0, 0)
    )
    pltpu.emit_pipeline(
        step,
        grid=(levels // LEVELS,),
        in_specs=[slab, next_level, slab, slab],
        out_specs=[slab],
        _explicit_indices=True,
    )(temp, temp, zonal, merid, out)


def settle_kernel(
    levels, sec, up_in, down_in, south_in, north_in, fresh_in, middle, blank,
    out,
    up, down, south, north, fresh, field, northmost, southmost, side_sem, in_sem, out_sem,
):
    rows, cells = field.shape[1:]
    patches = cells // 128

    @pl.when(sec[0] != 0)
    def _():
        pairs = (
            (up_in, up), (down_in, down), (south_in, south), (north_in, north), (fresh_in, fresh)
        )
        sides = [pltpu.make_async_copy(*pair, side_sem.at[n]) for n, pair in enumerate(pairs)]
        parts = [pl.ds(n * LEVELS, LEVELS) for n in range(levels // LEVELS)]
        ins = [
            pltpu.make_async_copy(middle.at[0, part], field.at[part], in_sem.at[n])
            for n, part in enumerate(parts)
        ]
        outs = [
            pltpu.make_async_copy(field.at[part], out.at[0, part], out_sem.at[n])
            for n, part in enumerate(parts)
        ]
        for copy in sides + ins:
            copy.start()
        for copy in sides:
            copy.wait()
        own_n = up[2 * levels : 2 * levels + 1, :].astype(i32)
        own_s = down[2 * levels : 2 * levels + 1, :].astype(i32)
        d_n = jnp.minimum(own_n, north[2 * levels : 2 * levels + 1, :].astype(i32))
        d_s = jnp.minimum(own_s, south[2 * levels : 2 * levels + 1, :].astype(i32))
        for at in range(0, levels, 8):
            k = iota((8, cells), 0) + at
            t, v = slice(at, at + 8), slice(levels + at, levels + at + 8)
            northmost[t, :] = through(k, d_n, up[t, :], north[t, :], up[v, :], north[v, :])
            southmost[t, :] = through(k, d_s, south[t, :], down[t, :], south[v, :], down[v, :])
        for n in range(len(parts)):
            ins[n].wait()
            for k in range(n * LEVELS, (n + 1) * LEVELS):
                field[k, rows - 1 : rows, :] += northmost[k : k + 1, :]
                field[k, 0:1, :] -= southmost[k : k + 1, :]
            if n == 0:
                for p in range(patches):
                    field[0, :, p * 128 : p * 128 + 128] = fresh[pl.ds(p, rows, stride=patches), :]
            outs[n].start()
        for copy in outs:
            copy.wait()


def in_three(x):
    high = x.astype(bf16)
    rest = x - high.astype(f32)
    middle = rest.astype(bf16)
    low = (rest - middle.astype(f32)).astype(bf16)
    return jnp.concatenate([high, middle, low], axis=1)


def joined(x, at=0):
    return x[:, at : at + 128] + (x[:, at + 128 : at + 256] + x[:, at + 256 : at + 384])


def heat_kernel(tiles, sec, payload, top, table, ret, fresh, hit, weighted):
    slots = tiles * CAPACITY

    @pl.when(sec[0] != 0)
    def _():
        ret[...] = jnp.zeros_like(ret)
        fresh[...] = jnp.zeros_like(fresh)

    @pl.when(sec[0] == 0)
    def _():
        surface_parts = in_three(top[0])
        table_parts = in_three(
            jnp.concatenate([table[...], jnp.zeros((128 - table.shape[0], 128), f32)], axis=0)
        )
        lane = iota((1, 4, 128), 2).astype(f32)
        group = min(64, tiles)

        def step(g, _):
            base = pl.multiple_of(g * group, group)
            upper = payload[pl.ds(base * CHUNK, group * CHUNK)].reshape(group, CHUNK, 4, 128)
            entry = upper[:, CAPACITY]
            at = pl.multiple_of(base * CAPACITY, group * CAPACITY)
            size = group * CAPACITY

            def named(offset):
                return jnp.concatenate(
                    [
                        jnp.where(
                            entry[:, None, :, 32 * q + offset : 32 * q + offset + 1] == lane[None],
                            1.0, 0.0,
                        )
                        for q in range(4)
                    ],
                    axis=1,
                ).reshape(size, 128)

            block_hit = named(0)
            block_one = block_hit.astype(bf16)
            row_one = named(16).astype(bf16)
            live = jnp.sum(block_hit, axis=1, keepdims=True) > 0
            hit[pl.ds(at, size), :] = block_one
            surface = joined(jnp.dot(block_one, surface_parts, preferred_element_type=f32))
            weights = joined(jnp.dot(row_one, table_parts, preferred_element_type=f32))

            def channel(c):
                return upper[:, :CAPACITY, c, :].reshape(size, 128)

            contrast = surface - channel(1)
            transfer = 0.8 + 0.4 * jnp.tanh(contrast)
            saturation = 0.6 * jnp.exp(0.3 * surface)
            heat = channel(3) - transfer * channel(0) * (
                contrast + 1.5 * (saturation - channel(2))
            )
            product = jnp.where(live, weights * heat, 0.0)
            weighted[pl.ds(at, size), 0:384] = in_three(product)
            weighted[pl.ds(at, size), 384:768] = in_three(weights)
            return 0

        lax.fori_loop(0, tiles // group, step, 0)
        sums = lax.dot_general(
            hit[...], weighted[...], (((0,), (0,)), ((), ())), preferred_element_type=f32
        )
        forcing = joined(sums) / jnp.maximum(joined(sums, 384), 1.0)
        new_top = top[1] + top[2] * forcing
        fresh[...] = new_top
        ret[...] = joined(jnp.dot(hit[...], in_three(new_top), preferred_element_type=f32))


def nothing_kernel(*refs):
    pass


def body(
    atm_state, routes, dst_block, weight_index, area_table, ocean_temp, vel_u, vel_v, depth_levels
):
    tiles = lax.axis_size("tile")
    block_count = atm_state.shape[1]
    levels, rows, cells = ocean_temp.shape[1:]
    patches = rows * cells // 128
    slots = tiles * CAPACITY
    sec = lax.axis_index("sec").astype(i32).reshape(1)
    grant = pltpu.CompilerParams(vmem_limit_bytes=24 << 20)
    ocean_grant = pltpu.CompilerParams(vmem_limit_bytes=56 << 20)
    whole_grant = pltpu.CompilerParams(vmem_limit_bytes=60 << 20)

    edge_rows = 2 * levels + 8
    payload, slot_of, up, down, brief_up, brief_down, blank = pl.pallas_call(
        functools.partial(pack_kernel, tiles),
        out_shape=(
            jax.ShapeDtypeStruct((tiles * CHUNK, 4, 128), f32),
            jax.ShapeDtypeStruct((block_count,), i32),
            jax.ShapeDtypeStruct((edge_rows, cells), f32),
            jax.ShapeDtypeStruct((edge_rows, cells), f32),
            jax.ShapeDtypeStruct((8, cells), f32),
            jax.ShapeDtypeStruct((8, cells), f32),
            jax.ShapeDtypeStruct(ocean_temp.shape, f32),
        ),
        in_specs=[SMEM] + [HBM] * 7,
        out_specs=(VMEM, SMEM, VMEM, VMEM, VMEM, VMEM, HBM),
        scratch_shapes=[
            pltpu.SMEM((block_count,), i32),
            pltpu.SMEM((block_count,), i32),
            pltpu.SMEM((block_count,), i32),
            pltpu.VMEM((block_count, 4, 128), f32),
            pltpu.SMEM((tiles,), i32),
            pltpu.VMEM((tiles * CHUNK, 128), i32),
            pltpu.VMEM((4, levels, 8, cells), f32),
            pltpu.VMEM((rows, cells), i32),
            pltpu.VMEM((LEVELS, rows, cells), f32),
            pltpu.SemaphoreType.DMA((3,)),
            pltpu.SemaphoreType.DMA((8,)),
            pltpu.SemaphoreType.DMA((4,)),
            pltpu.SemaphoreType.DMA((levels // LEVELS,)),
        ],
        compiler_params=whole_grant,
        name="pack",
    )(
        sec, routes.reshape(block_count), dst_block.reshape(block_count),
        weight_index.reshape(block_count), atm_state, depth_levels, ocean_temp, vel_v,
    )

    def unwritten(shapes):
        return pl.pallas_call(
            nothing_kernel,
            out_shape=shapes,
            out_specs=tuple(HBM for _ in shapes),
            compiler_params=ocean_grant,
            name="nothing",
        )()

    def from_sides(northmost, southmost):
        north_to = [(tiles + t, tiles + t + 1) for t in range(tiles - 1)]
        south_to = [(t + 1, t) for t in range(tiles, 2 * tiles - 1)]
        return (
            lax.ppermute(northmost, ("sec", "tile"), north_to),
            lax.ppermute(southmost, ("sec", "tile"), south_to),
        )

    top_shape = jax.ShapeDtypeStruct((3, patches, 128), f32)
    edge_shape = jax.ShapeDtypeStruct((edge_rows, cells), f32)
    field_shape = jax.ShapeDtypeStruct(ocean_temp.shape, f32)

    def split(atmosphere, ocean, *values):
        return lax.cond(sec[0] == 0, atmosphere, ocean, *values)

    def exchanged(value):
        return lax.all_to_all(value, "tile", split_axis=0, concat_axis=0, tiled=True)

    def surface(brief_up, brief_down):
        south, north = from_sides(brief_up, brief_down)
        return pl.pallas_call(
            surface_kernel,
            out_shape=top_shape,
            in_specs=[SMEM] + [HBM] * 4 + [ANY] * 2,
            out_specs=HBM,
            scratch_shapes=[
                pltpu.VMEM((2, rows, cells), f32),
                pltpu.VMEM((rows, cells), f32),
                pltpu.VMEM((rows, cells), f32),
                pltpu.VMEM((rows, cells), i32),
                pltpu.VMEM((2, 8, cells), f32),
                pltpu.VMEM((3, patches, 128), f32),
                pltpu.SemaphoreType.DMA((6,)),
                pltpu.SemaphoreType.DMA(()),
            ],
            compiler_params=ocean_grant,
            name="surface",
        )(sec, ocean_temp, vel_u, vel_v, depth_levels, south, north)

    def middle_of(temp, zonal, merid, depth):
        return pl.pallas_call(
            functools.partial(ocean_kernel, levels),
            in_specs=[HBM] * 4,
            out_specs=HBM,
            out_shape=field_shape,
            scratch_shapes=[
                pltpu.VMEM((rows, cells), i32),
                pltpu.VMEM((rows, cells), i32),
                pltpu.VMEM((rows, cells), i32),
                pltpu.VMEM((rows, cells), f32),
                pltpu.SemaphoreType.DMA(()),
            ],
            compiler_params=ocean_grant,
            name="ocean",
        )(temp, zonal, merid, depth)

    top = split(
        lambda up, down: unwritten((top_shape,))[0], surface, brief_up, brief_down
    )
    payload, up, down, top = lax.optimization_barrier((payload, up, down, top))
    top = lax.ppermute(top, "sec", [(1, 0)])

    def first_atmosphere(payload):
        payload, middle = lax.optimization_barrier((payload, unwritten((field_shape,))[0]))
        return exchanged(payload), middle

    moved, middle = split(
        first_atmosphere,
        lambda payload: (payload, middle_of(ocean_temp, vel_u, vel_v, depth_levels)),
        payload,
    )

    ret, fresh = pl.pallas_call(
        functools.partial(heat_kernel, tiles),
        out_shape=(
            jax.ShapeDtypeStruct((slots, 128), f32),
            jax.ShapeDtypeStruct((patches, 128), f32),
        ),
        in_specs=[SMEM, VMEM, VMEM, VMEM],
        out_specs=(VMEM, VMEM),
        scratch_shapes=[pltpu.VMEM((slots, 128), bf16), pltpu.VMEM((slots, 768), bf16)],
        compiler_params=grant,
        name="heat",
    )(sec, moved, top, area_table)
    fresh = lax.ppermute(fresh, "sec", [(0, 1)])

    def second_atmosphere(ret, up, down):
        ret, south, north = lax.optimization_barrier((ret, *unwritten((edge_shape, edge_shape))))
        return exchanged(ret), south, north

    back, south, north = split(
        second_atmosphere, lambda ret, up, down: (ret, *from_sides(up, down)), ret, up, down
    )
    index = slot_of - (CHUNK - CAPACITY) * (slot_of // CHUNK)
    whole_rows = lax.GatherDimensionNumbers(
        offset_dims=(1,), collapsed_slice_dims=(0,), start_index_map=(0,)
    )
    skin = split(
        lambda back, index: lax.gather(
            back, index[:, None], whole_rows, (1, 128),
            mode=lax.GatherScatterMode.PROMISE_IN_BOUNDS,
        ),
        lambda back, index: back[:block_count],
        back, index,
    )
    following = pl.pallas_call(
        functools.partial(settle_kernel, levels),
        out_shape=field_shape,
        in_specs=[SMEM] + [ANY] * 5 + [HBM] * 2,
        out_specs=HBM,
        scratch_shapes=[pltpu.VMEM((edge_rows, cells), f32)] * 4
        + [
            pltpu.VMEM((patches, 128), f32),
            pltpu.VMEM((levels, rows, cells), f32),
            pltpu.VMEM((levels, cells), f32),
            pltpu.VMEM((levels, cells), f32),
            pltpu.SemaphoreType.DMA((5,)),
            pltpu.SemaphoreType.DMA((levels // LEVELS,)),
            pltpu.SemaphoreType.DMA((levels // LEVELS,)),
        ],
        input_output_aliases={7: 0},
        compiler_params=grant,
        name="settle",
    )(sec, up, down, south, north, fresh, middle, blank)
    return following, skin[None]


def solution(mesh):
    return jax.shard_map(
        body,
        mesh=mesh,
        in_specs=(
            P("sec", "tile", None, None),
            P("sec", "tile", None),
            P("sec", "tile"),
            P("sec", "tile"),
            P(),
            P("sec", None, "tile", None),
            P("sec", None, "tile", None),
            P("sec", None, "tile", None),
            P("sec", "tile", None),
        ),
        out_specs=(P("sec", None, "tile", None), P("sec", "tile", None)),
        check_vma=False,
    )
```
